128 devices in a mesh: seq: 16 (over x_hi, y, core), grp: 8 (over x_lo, z).
Axes of the slice: x: 4 (x_hi: 2, x_lo: 2; x = x_hi * 2 + x_lo), y: 4, z: 4, core: 2. Of those that a mesh axis runs over, the one named last changes fastest.
Arguments:
- tokens: bfloat16 [1024, 32, 2048], P('grp', 'seq'), may hold values from -6 to 6
- norm_gain: float32 [2048], replicated, may hold values from 0.25 to 1.75
- qk_gain: float32 [2, 2, 16, 128], P(None, None, 'grp'), may hold values from 0.5 to 12
- window_blocks: int32 [8, 4], replicated, may hold values from 0 to 7, as said below
- w_spatial: bfloat16 [2048, 3, 2048], P('seq', None, 'grp'), may hold values from -0.13258252 to 0.13258252
- w_temporal: bfloat16 [2048, 3, 2048], P('seq', None, 'grp'), may hold values from -0.13258252 to 0.13258252
- w_out: bfloat16 [2048, 2, 2048], P('seq', None, 'grp'), may hold values from -0.09375 to 0.09375
Outputs:
- block_out: bfloat16 [1024, 32, 2048], P('grp', 'seq')
The draws below stay inside these ranges and needn't reach their ends.
Inputs may be any that keep to these rules, and one draw needn't show every extreme that they name: `window_blocks`: row t lists 4 distinct tiles, the first of them t itself.
All inputs are finite; a program needn't handle non-finite values.
Results may differ from the reference program's by a relative error of at most 0.015.
Values may be sent and summed in bfloat16 or wider, within the bound.
A program may use at most 128 MiB of HBM per device.

```python
import jax
import jax.numpy as jnp
from jax import lax

D = 2048
HEADS = 16
HD = 128
P_SIZE = 1024
TILE = 128
NB = 4
F = 32
HEADS_DEV = 2
NT = 8
N_GRP = 8


def attention_weight(key, marker):
    column_count = HEADS * HD
    base_draw = jnp.clip(jax.random.normal(jax.random.fold_in(key, marker), (D, 3, column_count), jnp.float32), -6.0, 6.0)
    return (base_draw * D ** (-0.5)).astype(jnp.bfloat16)


def draw_w_spatial(key, part):
    return attention_weight(key, 11)


def draw_w_temporal(key, part):
    return attention_weight(key, 23)


def draw_qk_gain(key, part):
    return jax.random.uniform(jax.random.fold_in(key, 33), (2, 2, HEADS, HD), jnp.float32, 0.5, 2.0)


def draw_window_blocks(key, part):
    row_keys = jax.random.split(jax.random.fold_in(key, 41), NT)

    def one_row(row_key, own_tile):
        others = jax.random.permutation(row_key, NT - 1)[:NB - 1]
        return jnp.concatenate([own_tile[None], (own_tile + 1 + others) % NT]).astype(jnp.int32)
    return jax.vmap(one_row)(row_keys, jnp.arange(NT, dtype=jnp.int32))


def block_scale(stream_key, dims, pieces, smallest, top_value):
    def one(dim, parts):
        heights = jax.random.uniform(jax.random.fold_in(jax.random.fold_in(stream_key, 6), dim), (parts,), jnp.float32, smallest / len(pieces), top_value / len(pieces))
        return jnp.repeat(jnp.exp(heights), dims[dim] // parts).reshape((-1,) + (1,) * (len(dims) - dim - 1))

    level = one(*pieces[0])
    for cut in pieces[1:]:
        level = level * one(*cut)
    return level


def centred(key, extent, width, most, cuts=(), held_as=jnp.bfloat16):
    factor_of = block_scale(key, extent, cuts, -0.22, 0.18) if cuts else 1.0
    result = jax.random.normal(key, extent, jnp.float32) * width * factor_of
    return jnp.minimum(jnp.maximum(result, -most), most).astype(held_as)


def setup_inputs(seed: int = 0) -> dict:
    key_of = jax.random.split(jax.random.key(seed), 8)
    tokens = centred(key_of[0], (P_SIZE, F, D), 1.0, 6.0, ((0, 8), (1, 16)))
    norm_gain = jnp.clip(1.0 + 0.15 * jax.random.normal(key_of[1], (D,), jnp.float32), 0.25, 1.75)
    qk_gain = draw_qk_gain(jax.random.fold_in(key_of[7], 71), 0)
    window_blocks = draw_window_blocks(jax.random.fold_in(key_of[7], 71), 0)
    w_spatial = draw_w_spatial(jax.random.fold_in(key_of[7], 71), 0)
    w_temporal = draw_w_temporal(jax.random.fold_in(key_of[7], 71), 0)
    w_out = centred(key_of[6], (D, 2, HEADS * HD), (2 * HEADS * HD) ** -0.5, 0.09375, ((0, 16), (2, 8)))
    return {"tokens": tokens, "norm_gain": norm_gain, "qk_gain": qk_gain, "window_blocks": window_blocks, "w_spatial": w_spatial, "w_temporal": w_temporal, "w_out": w_out}


def rms_scale(values):
    return values * lax.rsqrt(lax.optimization_barrier(jnp.mean(values * values, axis=-1, keepdims=True)) + 1e-06)

def finish_heads(projected, gain_pair, head_count):
    head_width = gain_pair.shape[-1]
    shaped = projected.reshape(projected.shape[0], projected.shape[1], 3, head_count, head_width)
    queries = (rms_scale(shaped[:, :, 0]) * gain_pair[0] * head_width ** (-0.5)).astype(jnp.bfloat16)
    key_rows = (rms_scale(shaped[:, :, 1]) * gain_pair[1]).astype(jnp.bfloat16)
    values = shaped[:, :, 2].astype(jnp.bfloat16)
    return (queries, key_rows, values)

def spatial_attention(queries, key_rows, values, window_blocks, tile_rows):
    row_total, frames, head_count, head_width = queries.shape
    tile_count = row_total // tile_rows
    listed = window_blocks.shape[1]
    query_tiles = queries.reshape(tile_count, tile_rows, frames, head_count, head_width).astype(jnp.float32)
    key_tiles = key_rows.reshape(tile_count, tile_rows, frames, head_count, head_width)[window_blocks]
    key_tiles = key_tiles.reshape(tile_count, listed * tile_rows, frames, head_count, head_width).astype(jnp.float32)
    value_tiles = values.reshape(tile_count, tile_rows, frames, head_count, head_width)[window_blocks]
    value_tiles = value_tiles.reshape(tile_count, listed * tile_rows, frames, head_count, head_width).astype(jnp.float32)
    scores = jnp.einsum('tqfhe,tkfhe->tfhqk', query_tiles, key_tiles)
    scores = jnp.exp(scores - lax.optimization_barrier(jnp.max(scores, axis=-1, keepdims=True)))
    attn_weights = (scores / lax.optimization_barrier(jnp.sum(scores, axis=-1, keepdims=True))).astype(jnp.bfloat16)
    attended = jnp.einsum('tfhqk,tkfhe->tqfhe', attn_weights.astype(jnp.float32), value_tiles)
    return attended.astype(jnp.bfloat16).reshape(row_total, frames, head_count, head_width)

def temporal_attention(queries, key_rows, values):
    frames = queries.shape[1]
    scores = jnp.einsum('rfhe,rghe->rhfg', queries.astype(jnp.float32), key_rows.astype(jnp.float32))
    causal = lax.broadcasted_iota(jnp.int32, (frames, frames), 1) <= lax.broadcasted_iota(jnp.int32, (frames, frames), 0)
    scores = jnp.where(causal, scores, jnp.float32(-1e+30))
    scores = jnp.exp(scores - lax.optimization_barrier(jnp.max(scores, axis=-1, keepdims=True)))
    attn_weights = (scores / lax.optimization_barrier(jnp.sum(scores, axis=-1, keepdims=True))).astype(jnp.bfloat16)
    attended = jnp.einsum('rhfg,rghe->rfhe', attn_weights.astype(jnp.float32), values.astype(jnp.float32))
    return attended.astype(jnp.bfloat16)

def reference(tokens, norm_gain, qk_gain, window_blocks, w_spatial, w_temporal, w_out):
    normed = (rms_scale(tokens.astype(jnp.float32)) * norm_gain).astype(jnp.bfloat16)
    flattened = normed.reshape(P_SIZE * F, D)
    spatial_proj = jnp.dot(flattened, w_spatial.reshape(D, 3 * HEADS * HD), preferred_element_type=jnp.float32)
    spatial_q, spatial_k, spatial_v = finish_heads(spatial_proj.reshape(P_SIZE, F, 3 * HEADS * HD), qk_gain[0], HEADS)
    spatial_out = spatial_attention(spatial_q, spatial_k, spatial_v, window_blocks, TILE)
    temporal_proj = jnp.dot(flattened, w_temporal.reshape(D, 3 * HEADS * HD), preferred_element_type=jnp.float32)
    temporal_q, temporal_k, temporal_v = finish_heads(temporal_proj.reshape(P_SIZE, F, 3 * HEADS * HD), qk_gain[1], HEADS)
    temporal_out = temporal_attention(temporal_q, temporal_k, temporal_v)
    branch_out = jnp.stack([spatial_out, temporal_out], axis=2).reshape(P_SIZE, F, 2, N_GRP, HEADS_DEV * HD)
    grouped = w_out.reshape(D, 2, N_GRP, HEADS_DEV * HD)
    summed = jnp.zeros((P_SIZE, F, D), jnp.float32)
    for head_group in range(N_GRP):
        partial_sum = jnp.einsum('pfbc,dbc->pfd', branch_out[:, :, :, head_group].astype(jnp.float32), grouped[:, :, head_group].astype(jnp.float32))
        rounded = lax.optimization_barrier(partial_sum.astype(jnp.bfloat16))
        summed = summed + rounded.astype(jnp.float32)
    return (tokens.astype(jnp.float32) + summed).astype(jnp.bfloat16)
```

```python
import jax
import jax.numpy as jnp
from jax import lax
from jax.experimental import pallas as pl
from jax.experimental.pallas import tpu as pltpu
from jax.sharding import PartitionSpec as P

MESH = pl.DeviceIdType.MESH
EPS = 1e-06
F32 = jnp.float32
BF16 = jnp.bfloat16

TOK, WGT, OUTW, GAIN, RING_T, RING_W2, RING_WX, RING_O2, RING_OX, RS, FIN = (
    0, 4, 8, 10, 12, 18, 24, 30, 36, 42, 48,
)
SLOTS = 52


def mm(a, b):
    return jnp.dot(a, b, preferred_element_type=F32)


def mm_t(a, b):
    return lax.dot_general(a, b, (((1,), (1,)), ((), ())), preferred_element_type=F32)


def kernel(
    win, tok, norm_gain, gain, w_s, w_t, wo_s, wo_t, out,
    nrm, xs, wg, wo, gn, qkv, att, part, rs1, rs2, fin, snd, rcv,
):
    s, g = lax.axis_index("seq"), lax.axis_index("grp")
    c, y, xh = lax.rem(s, 2), lax.rem(lax.div(s, 2), 4), lax.div(s, 8)
    xl, z = lax.div(g, 4), lax.rem(g, 4)
    x = xh * 2 + xl
    nc = 1 - c
    unit = c * y + nc * z
    unit2 = nc * y + c * z

    def dev(xh_, y_, c_, xl_, z_):
        return ((xh_ * 4 + y_) * 2 + c_, xl_ * 4 + z_)

    def remote(src, dst, i, j, to):
        return pltpu.make_async_remote_copy(
            src_ref=src, dst_ref=dst, send_sem=snd.at[i], recv_sem=rcv.at[j],
            device_id=to, device_id_type=MESH,
        )

    sends = []

    def put(src, dst, i, j, to):
        mine = jnp.logical_and(to[0] == s, to[1] == g)
        copy = remote(src, dst, i, j, to)

        @pl.when(mine)
        def _():
            pltpu.make_async_copy(src, dst, rcv.at[j]).start()

        @pl.when(jnp.logical_not(mine))
        def _():
            copy.start()

        sends.append((copy, jnp.logical_not(mine)))

    def arrived(dst, j):
        pltpu.make_async_copy(dst, dst, rcv.at[j]).wait()

    def start(copy):
        copy.start()
        sends.append((copy, None))

    class Ring:
        def __init__(self, view, at, right, left, base):
            self.view, self.at, self.base = view, at, base
            self.right, self.left = right, left
            self.units = (at, lax.rem(at + 3, 4), lax.rem(at + 1, 4), lax.rem(at + 2, 4))

        def send(self, u, half, k, to):
            ref = self.view(self.units[u], half)
            start(remote(ref, ref, self.base + k, self.base + k, to))

        def begin(self):
            self.send(0, 0, 0, self.right)
            self.send(0, 1, 3, self.left)
            self.send(0, 1, 1, self.right)
            self.send(0, 0, 4, self.left)

        def forward(self):
            arrived(self.view(self.units[1], 0), self.base + 0)
            self.send(1, 0, 2, self.right)
            arrived(self.view(self.units[2], 1), self.base + 3)
            self.send(2, 1, 5, self.left)

        def near(self):
            arrived(self.view(self.units[1], 1), self.base + 1)
            arrived(self.view(self.units[2], 0), self.base + 4)

        def far(self):
            arrived(self.view(self.units[3], 0), self.base + 2)
            arrived(self.view(self.units[3], 1), self.base + 5)

    def along(dy, dz):
        return dev(xh, lax.rem(y + dy, 4), c, xl, lax.rem(z + dz, 4))

    def across(dx):
        nx = lax.rem(x + dx, 4)
        return dev(lax.div(nx, 2), y, c, lax.rem(nx, 2), z)

    right, left = along(c, nc), along(3 * c, 3 * nc)
    right2, left2 = along(nc, c), along(3 * nc, 3 * c)

    ring_t = Ring(lambda u, h: xs.at[u, pl.ds(h * 256, 256)], unit, right, left, RING_T)
    ring_w2 = Ring(
        lambda u, h: wg.at[x, pl.ds(u * 256 + h * 128, 128)], unit2, right2, left2, RING_W2
    )
    ring_wx = Ring(
        lambda u, h: wg.at[u, pl.ds(h * 512, 512)], x, across(1), across(3), RING_WX
    )
    ring_o2 = Ring(
        lambda u, h: wo.at[x, pl.ds(u * 256 + h * 128, 128)], unit2, right2, left2, RING_O2
    )
    ring_ox = Ring(
        lambda u, h: wo.at[u, pl.ds(h * 512, 512)], x, across(1), across(3), RING_OX
    )

    to_s, to_t = dev(xh, y, 0, xl, z), dev(xh, z, 1, xl, y)
    row_s = y * 256 + c * 128
    put(w_s, wg.at[x, pl.ds(row_s, 128)], WGT, WGT + c, to_s)
    put(w_t, wg.at[x, pl.ds(row_s, 128)], WGT + 1, WGT + c, to_t)

    for h in range(2):
        def norm_rows(k, _):
            rows = pl.ds(pl.multiple_of(h * 128 + k * 32, 32), 32)
            v = tok[rows, :].astype(F32)
            scale = lax.rsqrt(jnp.mean(v * v, axis=-1, keepdims=True) + EPS)
            nrm[rows, :] = (v * scale * norm_gain[...]).astype(BF16)
            return 0

        lax.fori_loop(0, 4, norm_rows, 0)
        src = nrm.at[pl.ds(h * 128, 128)]
        i_s, i_t = xl * 2 + h, xh * 2 + c
        put(src, xs.at[z, pl.ds(i_s * 128, 128)], TOK + h, TOK + i_s, dev(xh, y, 0, c, z))
        put(src, xs.at[y, pl.ds(i_t * 128, 128)], TOK + 2 + h, TOK + i_t, dev(h, y, 1, xl, z))

    put(wo_s, wo.at[x, pl.ds(row_s, 128)], OUTW, OUTW + c, to_s)
    put(wo_t, wo.at[x, pl.ds(row_s, 128)], OUTW + 1, OUTW + c, to_t)
    for h in range(2):
        put(
            gain.at[c], gn.at[xl], GAIN + h, GAIN + xl,
            dev(xh, nc * y + c * z, c, h, nc * z + c * y),
        )

    for i in range(2):
        arrived(wg.at[x, pl.ds(unit2 * 256 + i * 128, 128)], WGT + i)
    ring_w2.begin()
    for i in range(4):
        arrived(xs.at[unit, pl.ds(i * 128, 128)], TOK + i)
    ring_t.begin()
    ring_w2.forward()
    ring_w2.near()
    ring_w2.far()
    ring_wx.begin()
    for i in range(2):
        arrived(wo.at[x, pl.ds(unit2 * 256 + i * 128, 128)], OUTW + i)
        arrived(gn.at[i], GAIN + i)
    ring_o2.begin()
    ring_t.forward()
    ring_o2.forward()
    ring_o2.near()
    ring_o2.far()
    ring_wx.forward()
    ring_ox.begin()
    ring_t.near()
    ring_t.far()
    ring_wx.near()

    def project(pair):
        def one(u, _):
            for n in range(3):
                cols = slice(n * 256, n * 256 + 256)
                acc = mm(xs[u, :, 0:1024], wg[pair, :, cols])
                acc = acc + mm(xs[u, :, 1024:2048], wg[2 + pair, :, cols])
                for j in range(2):
                    a = acc[:, j * 128 : j * 128 + 128]
                    if n < 2:
                        a = a * lax.rsqrt(jnp.mean(a * a, axis=-1, keepdims=True) + EPS)
                        a = a * gn[pair, 2 * n + j : 2 * n + j + 1, :]
                    if n == 0:
                        a = a * (128 ** -0.5)
                    a = a.astype(BF16)
                    for k in range(8):
                        i, f = k // 2, k % 2
                        t = (i // 2) * 4 + u
                        to_row = nc * (f * 16 + t * 2 + i % 2) + c * (t * 4 + i % 2 * 2 + f)
                        qkv[n, pair * 2 + j, to_row] = a[k * 64 : k * 64 + 64]
            return 0

        lax.fori_loop(0, 4, one, 0)

    project(1 - xl)
    ring_ox.forward()
    ring_wx.far()
    project(xl)
    ring_ox.near()
    ring_ox.far()

    @pl.when(c == 0)
    def _():
        def spatial(ft, _):
            f, t = lax.div(ft, 8), lax.rem(ft, 8)
            at = [f * 16 + 2 * win[t, j] for j in range(4)]
            for hd in range(4):
                q = qkv[0, hd, pl.ds(f * 16 + 2 * t, 2)].reshape(128, 128)
                sc = [mm_t(q, qkv[1, hd, pl.ds(a, 2)].reshape(128, 128)) for a in at]
                top = jnp.maximum(jnp.maximum(sc[0], sc[1]), jnp.maximum(sc[2], sc[3]))
                top = jnp.max(top, axis=-1, keepdims=True)
                sc = [jnp.exp(v - top) for v in sc]
                total = jnp.sum(sc[0] + sc[1] + sc[2] + sc[3], axis=-1, keepdims=True)
                inv = 1.0 / total
                o = 0.0
                for v, a in zip(sc, at):
                    o = o + mm((v * inv).astype(BF16), qkv[2, hd, pl.ds(a, 2)].reshape(128, 128))
                o = o.astype(BF16)
                for h in range(2):
                    att[
                        lax.rem(t, 4), lax.div(t, 4) * 4 + h * 2 + f, :, hd * 128 : hd * 128 + 128
                    ] = o[h * 64 : h * 64 + 64]
            return 0

        lax.fori_loop(0, 16, spatial, 0)

    @pl.when(c == 1)
    def _():
        def temporal(pg, _):
            rows = pl.ds(pl.multiple_of(pg * 16, 16), 16)
            for hd in range(4):
                q, k, v = (qkv[n, hd, :, rows, :].reshape(512, 128) for n in range(3))
                for b in range(2):
                    keys = 256 * (b + 1)
                    sc = mm_t(q[b * 256 : b * 256 + 256], k[:keys])
                    qi = lax.broadcasted_iota(jnp.int32, (256, keys), 0) + b * 256
                    ki = lax.broadcasted_iota(jnp.int32, (256, keys), 1)
                    ok = jnp.logical_and(
                        jnp.bitwise_and(qi, 15) == jnp.bitwise_and(ki, 15), ki <= qi
                    )
                    sc = jnp.where(ok, sc, -1e30)
                    sc = jnp.exp(sc - jnp.max(sc, axis=-1, keepdims=True))
                    inv = 1.0 / jnp.sum(sc, axis=-1, keepdims=True)
                    o = mm((sc * inv).astype(BF16), v[:keys]).astype(BF16)
                    for m in range(16):
                        fr = b * 16 + m
                        t = fr // 4
                        i = (t // 4) * 2 + (fr // 2) % 2
                        att[t % 4, i * 2 + fr % 2, rows, hd * 128 : hd * 128 + 128] = o[
                            m * 16 : m * 16 + 16
                        ]
            return 0

        lax.fori_loop(0, 4, temporal, 0)

    def outproj(u):
        def one(k, _):
            o = att[u].reshape(512, 512)
            half, rows = lax.div(k, 4), pl.ds(pl.multiple_of(lax.rem(k, 4) * 256, 256), 256)
            acc = mm_t(o[:, 0:256], wo[half * 2, rows, :])
            acc = acc + mm_t(o[:, 256:512], wo[half * 2 + 1, rows, :])
            part[u, :, pl.ds(pl.multiple_of(k * 256, 256), 256)] = acc.astype(BF16)
            return 0

        lax.fori_loop(0, 8, one, 0)

    def add_rows(u, first, count, others):
        def one(k, _):
            rows = pl.ds(pl.multiple_of(first + k * 32, 32), 32)
            total = part[u, rows, :].astype(F32)
            for other, off in others:
                at = pl.ds(pl.multiple_of(first - off + k * 32, 32), 32)
                total = total + other[at, :].astype(F32)
            part[u, rows, :] = total.astype(BF16)
            return 0

        lax.fori_loop(0, count // 32, one, 0)

    A, B = pl.ds(0, 256), pl.ds(256, 256)
    u_l, u_r, u_2 = lax.rem(unit + 3, 4), lax.rem(unit + 1, 4), lax.rem(unit + 2, 4)
    outproj(u_2)
    start(remote(part.at[u_2, A], rs1.at[0], RS, RS, right))
    start(remote(part.at[u_2, B], rs1.at[1], RS + 1, RS + 1, left))
    outproj(u_r)
    start(remote(part.at[u_r, B], rs2.at[0, B], RS + 2, RS + 2, right))
    outproj(u_l)
    start(remote(part.at[u_l, A], rs2.at[1, A], RS + 3, RS + 3, left))
    arrived(rs1.at[0], RS)
    add_rows(u_r, 0, 256, [(rs1.at[0], 0)])
    start(remote(part.at[u_r, A], rs2.at[0, A], RS + 4, RS + 4, right))
    arrived(rs1.at[1], RS + 1)
    add_rows(u_l, 256, 256, [(rs1.at[1], 256)])
    start(remote(part.at[u_l, B], rs2.at[1, B], RS + 5, RS + 5, left))
    outproj(unit)

    def finish(i):
        a, b = i // 2, i % 2
        slot = nc * b + c * (2 + xh)
        to = dev(nc * xh + c * a, y, nc * xl + c * b, nc * a + c * xl, z)
        put(part.at[unit, pl.ds(i * 128, 128)], fin.at[slot], FIN + i, FIN + slot, to)

    arrived(rs2.at[0, B], RS + 2)
    arrived(rs2.at[1, A], RS + 3)
    arrived(rs2.at[0, A], RS + 4)
    add_rows(unit, 0, 256, [(rs2.at[0], 0), (rs2.at[1], 0)])
    finish(0)
    finish(1)
    arrived(rs2.at[1, B], RS + 5)
    add_rows(unit, 256, 256, [(rs2.at[0], 0), (rs2.at[1], 0)])
    finish(2)
    finish(3)

    for h in range(2):
        arrived(fin.at[h], FIN + h)
        arrived(fin.at[2 + h], FIN + 2 + h)

        def total_rows(k, _):
            rows = pl.ds(pl.multiple_of(k * 32, 32), 32)
            here = pl.ds(pl.multiple_of(h * 128 + k * 32, 32), 32)
            total = fin[h, rows, :].astype(F32) + fin[2 + h, rows, :].astype(F32)
            out[here, :] = (tok[here, :].astype(F32) + total).astype(BF16)
            return 0

        lax.fori_loop(0, 4, total_rows, 0)

    for copy, cond in sends:
        if cond is None:
            copy.wait_send()
        else:
            pl.when(cond)(copy.wait_send)


def body(tokens, norm_gain, qk_gain, window_blocks, w_spatial, w_temporal, w_out):
    rows, frames, width = tokens.shape
    tok = tokens.reshape(2, 64, 2, width).transpose(0, 2, 1, 3).reshape(256, width)
    vmem = pl.BlockSpec(memory_space=pltpu.VMEM)
    res = pl.pallas_call(
        kernel,
        name="attention_block",
        out_shape=jax.ShapeDtypeStruct((256, width), BF16),
        in_specs=[pl.BlockSpec(memory_space=pltpu.SMEM)] + [vmem] * 7,
        out_specs=vmem,
        scratch_shapes=[
            pltpu.VMEM((256, 2048), BF16),
            pltpu.VMEM((4, 512, 2048), BF16),
            pltpu.VMEM((4, 1024, 768), BF16),
            pltpu.VMEM((4, 1024, 256), BF16),
            pltpu.VMEM((2, 4, 128), F32),
            pltpu.VMEM((3, 4, 32, 64, 128), BF16),
            pltpu.VMEM((4, 8, 64, 512), BF16),
            pltpu.VMEM((4, 512, 2048), BF16),
            pltpu.VMEM((2, 256, 2048), BF16),
            pltpu.VMEM((2, 512, 2048), BF16),
            pltpu.VMEM((4, 128, 2048), BF16),
            pltpu.SemaphoreType.DMA((SLOTS,)),
            pltpu.SemaphoreType.DMA((SLOTS,)),
        ],
        compiler_params=pltpu.CompilerParams(
            has_side_effects=True, vmem_limit_bytes=60 * 1024 * 1024
        ),
    )(
        window_blocks,
        tok,
        norm_gain.reshape(1, width),
        qk_gain.reshape(2, 4, 128),
        w_spatial.reshape(128, 768),
        w_temporal.reshape(128, 768),
        w_out[:, 0, :],
        w_out[:, 1, :],
    )
    return res.reshape(2, 2, 64, width).transpose(0, 2, 1, 3).reshape(rows, frames, width)


def solution(mesh):
    return jax.shard_map(
        body,
        mesh=mesh,
        in_specs=(
            P("grp", "seq", None),
            P(),
            P(None, None, "grp", None),
            P(),
            P("seq", None, "grp"),
            P("seq", None, "grp"),
            P("seq", None, "grp"),
        ),
        out_specs=P("grp", "seq", None),
        check_vma=False,
    )
```

```python
import jax
import jax.numpy as jnp
from jax import lax
from jax.experimental import pallas as pl
from jax.experimental.pallas import tpu as pltpu
from jax.sharding import PartitionSpec as P

MESH = pl.DeviceIdType.MESH
EPS = 1e-06
F32 = jnp.float32
BF16 = jnp.bfloat16

TOK, WGT, OUTW, GAIN, RING_TL, RING_TR, RING_W, RING_O, RS, FIN = (
    0, 4, 6, 8, 10, 16, 22, 46, 70, 94,
)
SLOTS = 98


def mm(a, b):
    return jnp.dot(a, b, preferred_element_type=F32)


def mm_t(a, b):
    return lax.dot_general(a, b, (((1,), (1,)), ((), ())), preferred_element_type=F32)


def kernel(
    win, tok, norm_gain, gain, w_s, w_t, wo_s, wo_t, out,
    nrm, xs, wg, wo, gn, qkv, att, part, rs1, rs2, fin, snd, rcv,
):
    s, g = lax.axis_index("seq"), lax.axis_index("grp")
    c, y, xh = lax.rem(s, 2), lax.rem(lax.div(s, 2), 4), lax.div(s, 8)
    xl, z = lax.div(g, 4), lax.rem(g, 4)
    x = xh * 2 + xl
    nc = 1 - c
    unit = c * y + nc * z
    unit2 = nc * y + c * z
    local = nc * xl + c * xh

    def dev(xh_, y_, c_, xl_, z_):
        return ((xh_ * 4 + y_) * 2 + c_, xl_ * 4 + z_)

    def along(dy, dz):
        return dev(xh, lax.rem(y + dy, 4), c, xl, lax.rem(z + dz, 4))

    def across(dx):
        nx = lax.rem(x + dx, 4)
        return dev(lax.div(nx, 2), y, c, lax.rem(nx, 2), z)

    right, left = along(c, nc), along(3 * c, 3 * nc)
    right2, left2 = along(nc, c), along(3 * nc, 3 * c)
    right_x, left_x = across(1), across(3)

    barrier = pltpu.get_barrier_semaphore()
    peers = [right, left, right2, left2, right_x, left_x, dev(xh, y, nc, xl, z)]
    for b in range(2):
        peers.append(dev(xh, y, b, 1 - xl, z))
        peers.append(dev(1 - xh, y, b, xl, z))
        for a in range(2):
            peers.append(dev(xh, z, a, b, y))
    for to in peers:
        pl.semaphore_signal(barrier, inc=1, device_id=to, device_id_type=MESH)

    def remote(src, dst, i, j, to):
        return pltpu.make_async_remote_copy(
            src_ref=src, dst_ref=dst, send_sem=snd.at[i], recv_sem=rcv.at[j],
            device_id=to, device_id_type=MESH,
        )

    sends = []

    def put(src, dst, i, j, to):
        mine = jnp.logical_and(to[0] == s, to[1] == g)
        copy = remote(src, dst, i, j, to)

        @pl.when(mine)
        def _():
            pltpu.make_async_copy(src, dst, rcv.at[j]).start()

        @pl.when(jnp.logical_not(mine))
        def _():
            copy.start()

        sends.append((copy, jnp.logical_not(mine)))

    def arrived(dst, j):
        pltpu.make_async_copy(dst, dst, rcv.at[j]).wait()

    def start(copy):
        copy.start()
        sends.append((copy, None))

    class Ring:
        def __init__(self, view, at, to_right, to_left, base):
            self.view, self.base = view, base
            self.to = (to_right, to_left)
            self.units = (at, lax.rem(at + 3, 4), lax.rem(at + 1, 4), lax.rem(at + 2, 4))

        def send(self, u, half, k, side):
            ref = self.view(self.units[u], half)
            start(remote(ref, ref, self.base + k, self.base + k, self.to[side]))

        def wait(self, *slots):
            for k in slots:
                u, half = ((1, 0), (1, 1), (3, 0), (2, 1), (2, 0), (3, 1))[k]
                arrived(self.view(self.units[u], half), self.base + k)

        def begin(self):
            self.send(0, 0, 0, 0)
            self.send(0, 1, 3, 1)
            self.send(0, 1, 1, 0)
            self.send(0, 0, 4, 1)

        def forward(self):
            self.wait(0)
            self.send(1, 0, 2, 0)
            self.wait(3)
            self.send(2, 1, 5, 1)

    def token_ring(part_, base):
        return Ring(
            lambda u, h: xs.at[u, pl.ds((part_ * 2 + h) * 128, 128)], unit, right, left, base
        )

    def weight_rings(w, base):
        def both(u, h):
            pair = (1 - xl) if h == 0 else xl
            return w.at[pair, :, 1, :, pl.ds(u * 128, 128)]

        return (
            Ring(
                lambda u, h: w.at[xl, xh, 0, :, pl.ds(u * 128 + h * 64, 64)],
                unit2, right2, left2, base,
            ),
            Ring(
                lambda u, h: w.at[lax.rem(u, 2), lax.div(u, 2), 0, :, pl.ds(h * 256, 256)],
                x, right_x, left_x, base + 6,
            ),
            Ring(
                lambda u, h: w.at[
                    lax.rem(u, 2), lax.div(u, 2), 1, :, pl.ds(unit2 * 128 + h * 64, 64)
                ],
                x, right_x, left_x, base + 12,
            ),
            Ring(both, unit2, right2, left2, base + 18),
        )

    tok_l, tok_r = token_ring(local, RING_TL), token_ring(1 - local, RING_TR)
    w1a, w1b, w2a, w2b = weight_rings(wg, RING_W)
    o1a, o1b, o2a, o2b = weight_rings(wo, RING_O)

    def norm_half(h):
        def norm_rows(k, _):
            rows = pl.ds(pl.multiple_of(h * 128 + k * 32, 32), 32)
            v = tok[rows, :].astype(F32)
            scale = lax.rsqrt(jnp.mean(v * v, axis=-1, keepdims=True) + EPS)
            v = (v * scale * norm_gain[...]).astype(BF16)
            for old in range(16):
                new = (old // 8 * 2 + old % 2) * 4 + old // 2 % 4
                nrm[rows, new * 128 : new * 128 + 128] = v[:, old * 128 : old * 128 + 128]
            return 0

        lax.fori_loop(0, 4, norm_rows, 0)

    norm_half(0)
    norm_half(1)
    pl.semaphore_wait(barrier, len(peers))

    to_s, to_t = dev(xh, y, 0, xl, z), dev(xh, z, 1, xl, y)
    mine_w, mine_o = (w.at[xl, xh, c, :, pl.ds(y * 128, 128)] for w in (wg, wo))
    put(w_s, mine_w, WGT, WGT + c, to_s)
    put(w_t, mine_w, WGT + 1, WGT + c, to_t)
    for h in range(2):
        src = nrm.at[pl.ds(h * 128, 128)]
        i_s, i_t = xl * 2 + h, xh * 2 + c
        put(src, xs.at[z, pl.ds(i_s * 128, 128)], TOK + h, TOK + i_s, dev(xh, y, 0, c, z))
        put(src, xs.at[y, pl.ds(i_t * 128, 128)], TOK + 2 + h, TOK + i_t, dev(h, y, 1, xl, z))
    put(wo_s, mine_o, OUTW, OUTW + c, to_s)
    put(wo_t, mine_o, OUTW + 1, OUTW + c, to_t)
    for h in range(2):
        put(
            gain.at[c], gn.at[xl], GAIN + h, GAIN + xl,
            dev(xh, nc * y + c * z, c, h, nc * z + c * y),
        )

    def rows_arrived(w, i, slot):
        arrived(w.at[xl, xh, i, :, pl.ds(unit2 * 128, 128)], slot + i)

    def tokens_arrived(half):
        for h in range(2):
            i = half * 2 + h
            arrived(xs.at[unit, pl.ds(i * 128, 128)], TOK + i)

    rows_arrived(wg, 0, WGT)
    w1a.begin()
    tokens_arrived(local)
    tok_l.begin()
    rows_arrived(wg, 1, WGT)
    w2a.begin()
    w1a.forward()
    w2a.forward()
    w1a.wait(1, 4, 2, 5)
    w1b.begin()
    w2a.wait(1, 4, 2, 5)
    w2b.begin()
    tok_l.forward()
    tokens_arrived(1 - local)
    tok_r.begin()
    w1b.forward()
    w2b.forward()
    tok_r.forward()
    tok_l.wait(1, 4, 2, 5)
    for i in range(2):
        arrived(gn.at[i], GAIN + i)
    tok_r.wait(1, 4, 2, 5)
    w1b.wait(1, 4)
    w2b.wait(1, 4, 2)
    for i in range(2):
        rows_arrived(wo, i, OUTW)
    o1a.begin()
    o2a.begin()

    def project(pair):
        def one(u, _):
            w = [wg[pair, :, :, n].reshape(2048, 256) for n in range(3)]
            acc = mm(xs[u], jnp.concatenate(w, axis=1))
            for n in range(3):
                for j in range(2):
                    a = acc[:, n * 256 + j * 128 : n * 256 + j * 128 + 128]
                    if n < 2:
                        a = a * lax.rsqrt(jnp.mean(a * a, axis=-1, keepdims=True) + EPS)
                        a = a * gn[pair, 2 * n + j : 2 * n + j + 1, :]
                    if n == 0:
                        a = a * (128 ** -0.5)

                    @pl.when(c == 0)
                    def _():
                        b = a.astype(BF16)
                        for k in range(8):
                            i, f = k // 2, k % 2
                            first = f * 64 + ((i // 2) * 4 + u) * 8 + i % 2 * 4
                            qkv[n, pair * 2 + j, pl.ds(first, 4)] = b[
                                k * 64 : k * 64 + 64
                            ].reshape(4, 16, 128)

                    @pl.when(c == 1)
                    def _():
                        for i in range(4):
                            for m in range(8):
                                at = i * 128 + m * 8
                                b = jnp.concatenate([a[at : at + 8], a[at + 64 : at + 72]], axis=0)
                                at = m * 16 + ((i // 2) * 4 + u) * 2 + i % 2
                                qkv[n, pair * 2 + j, at] = b.astype(BF16)
            return 0

        lax.fori_loop(0, 4, one, 0)

    def softmax_mix(sc, v):
        e = jnp.exp(sc - jnp.max(sc, axis=-1, keepdims=True)).astype(BF16)
        o = mm(e, jnp.concatenate([v, jnp.ones_like(v)], axis=1))
        return o[:, 0:128] / o[:, 128:256]

    def tile(n, hd, first, rows=128):
        return qkv[n, hd, pl.ds(first, rows // 16)].reshape(rows, 128)

    def attend(pair, half):
        @pl.when(c == 0)
        def _():
            def spatial(k, _):
                t = half * 4 + k
                for f in range(2):
                    at = [f * 64 + win[j, t] * 8 for j in range(4)]
                    for j in range(2):
                        hd = pair * 2 + j
                        q = tile(0, hd, f * 64 + t * 8)
                        keys = jnp.concatenate([tile(1, hd, a) for a in at], axis=0)
                        vals = jnp.concatenate([tile(2, hd, a) for a in at], axis=0)
                        o = softmax_mix(mm_t(q, keys), vals).astype(BF16)
                        for h in range(2):
                            att[
                                pair, k, half * 4 + h * 2 + f, :, j * 128 : j * 128 + 128
                            ] = o[h * 64 : h * 64 + 64]
                return 0

            lax.fori_loop(0, 4, spatial, 0)

        for b in range(2):
            @pl.when(jnp.logical_and(c == 1, half == b))
            def _():
                def temporal(pg, _):
                    rows = pl.ds(pl.multiple_of(pg * 16, 16), 16)
                    keys = 128 * (b + 1)
                    qi = lax.broadcasted_iota(jnp.int32, (128, keys), 0) + b * 128
                    ki = lax.broadcasted_iota(jnp.int32, (128, keys), 1)
                    ok = jnp.logical_and(
                        jnp.bitwise_and(qi, 7) == jnp.bitwise_and(ki, 7), ki <= qi
                    )
                    for j in range(2):
                        hd = pair * 2 + j
                        res = []
                        for m in range(2):
                            first = pg * 32 + m * 16
                            q = tile(0, hd, first + b * 8)
                            sc = mm_t(q, tile(1, hd, first, keys))
                            res.append(
                                softmax_mix(jnp.where(ok, sc, -1e30), tile(2, hd, first, keys))
                            )
                        for m in range(16):
                            fr = b * 16 + m
                            i = b * 2 + (fr // 2) % 2
                            o = jnp.concatenate([v[m * 8 : m * 8 + 8] for v in res], axis=0)
                            att[
                                pair, fr // 4 % 4, i * 2 + fr % 2, rows, j * 128 : j * 128 + 128
                            ] = o.astype(BF16)
                    return 0

                lax.fori_loop(0, 4, temporal, 0)

    project(1 - xl)
    o1a.forward()
    o2a.forward()
    attend(1 - xl, 0)
    o1a.wait(1, 4, 2, 5)
    o1b.begin()
    o2a.wait(1, 4, 2, 5)
    o2b.begin()
    attend(1 - xl, 1)
    w1b.wait(2, 5)
    w2b.wait(5)
    o1b.forward()
    o2b.forward()
    project(xl)
    attend(xl, 1 - local)
    o1b.wait(1, 4, 2, 5)
    o2b.wait(1, 4, 2, 5)

    def outproj(u, half):
        def one(k, _):
            rows = pl.ds(pl.multiple_of(half * 256, 256), 256)
            o = [att[p, u, pl.ds(half * 4, 4)].reshape(256, 256) for p in range(2)]
            for b in range(2):
                acc = mm_t(o[0], wo[0, k, b, 0]) + mm_t(o[1], wo[1, k, b, 0])
                for q in range(4):
                    cols = pl.ds(pl.multiple_of(k * 1024 + q * 256 + b * 128, 128), 128)
                    part[u, rows, cols] = acc[:, q * 128 : q * 128 + 128].astype(BF16)
            return 0

        lax.fori_loop(0, 2, one, 0)

    def add_rows(u, first, *others):
        def one(k, _):
            rows = pl.ds(pl.multiple_of(first + k * 32, 32), 32)
            here = pl.ds(pl.multiple_of(k * 32, 32), 32)
            total = part[u, rows, :].astype(F32)
            for other in others:
                total = total + other[here, :].astype(F32)
            part[u, rows, :] = total.astype(BF16)
            return 0

        lax.fori_loop(0, 2, one, 0)

    u_l, u_r, u_2 = lax.rem(unit + 3, 4), lax.rem(unit + 1, 4), lax.rem(unit + 2, 4)
    pieces = [(1 - local) * 2, (1 - local) * 2 + 1, local * 2, local * 2 + 1]

    def reduce_send(n, u, q, dst, k, to):
        src = part.at[u, pl.ds(pieces[n] * 128 + q * 64, 64)]
        start(remote(src, dst, RS + n * 6 + k, RS + n * 6 + k, to))

    def reduce_start(half, n):
        outproj(u_2, half)
        reduce_send(n, u_2, 0, rs1.at[n, 0], 0, right)
        reduce_send(n, u_2, 1, rs1.at[n, 1], 1, left)
        outproj(u_r, half)
        reduce_send(n, u_r, 1, rs2.at[n, 0, 1], 2, right)
        outproj(u_l, half)
        reduce_send(n, u_l, 0, rs2.at[n, 1, 0], 3, left)
        reduce_send(n + 1, u_2, 0, rs1.at[n + 1, 0], 0, right)
        reduce_send(n + 1, u_2, 1, rs1.at[n + 1, 1], 1, left)
        reduce_send(n + 1, u_r, 1, rs2.at[n + 1, 0, 1], 2, right)
        reduce_send(n + 1, u_l, 0, rs2.at[n + 1, 1, 0], 3, left)

    def reduce_pass(n):
        arrived(rs1.at[n, 0], RS + n * 6)
        add_rows(u_r, pieces[n] * 128, rs1.at[n, 0])
        reduce_send(n, u_r, 0, rs2.at[n, 0, 0], 4, right)
        arrived(rs1.at[n, 1], RS + n * 6 + 1)
        add_rows(u_l, pieces[n] * 128 + 64, rs1.at[n, 1])
        reduce_send(n, u_l, 1, rs2.at[n, 1, 1], 5, left)

    def reduce_end(half, n):
        h = n % 2
        for q in range(2):
            arrived(rs2.at[n, 1 - q, q], RS + n * 6 + 3 - q)
            arrived(rs2.at[n, q, q], RS + n * 6 + 4 + q)
            add_rows(unit, pieces[n] * 128 + q * 64, rs2.at[n, 0, q], rs2.at[n, 1, q])
        at = nc * h + c * (2 + xh)
        to = dev(nc * xh + c * half, y, nc * xl + c * h, nc * half + c * xl, z)
        put(part.at[unit, pl.ds(pieces[n] * 128, 128)], fin.at[at], FIN + n, FIN + at, to)

    reduce_start(1 - local, 0)
    attend(xl, local)
    reduce_pass(0)
    reduce_pass(1)
    outproj(unit, 1 - local)
    reduce_start(local, 2)
    reduce_end(1 - local, 0)
    reduce_end(1 - local, 1)
    reduce_pass(2)
    reduce_pass(3)
    outproj(unit, local)
    reduce_end(local, 2)
    reduce_end(local, 3)

    for h in range(2):
        arrived(fin.at[h], FIN + h)
        arrived(fin.at[2 + h], FIN + 2 + h)

        def total_rows(k, _):
            rows = pl.ds(pl.multiple_of(k * 32, 32), 32)
            here = pl.ds(pl.multiple_of(h * 128 + k * 32, 32), 32)
            total = fin[h, rows, :].astype(F32) + fin[2 + h, rows, :].astype(F32)
            out[here, :] = (tok[here, :].astype(F32) + total).astype(BF16)
            return 0

        lax.fori_loop(0, 4, total_rows, 0)

    for copy, cond in sends:
        if cond is None:
            copy.wait_send()
        else:
            pl.when(cond)(copy.wait_send)


def body(tokens, norm_gain, qk_gain, window_blocks, w_spatial, w_temporal, w_out):
    rows, frames, width = tokens.shape
    tok = tokens.reshape(2, 64, 2, width).transpose(0, 2, 1, 3).reshape(256, width)
    vmem = pl.BlockSpec(memory_space=pltpu.VMEM)
    res = pl.pallas_call(
        kernel,
        name="attention_block",
        out_shape=jax.ShapeDtypeStruct((256, width), BF16),
        in_specs=[pl.BlockSpec(memory_space=pltpu.SMEM)] + [vmem] * 7,
        out_specs=vmem,
        scratch_shapes=[
            pltpu.VMEM((256, 2048), BF16),
            pltpu.VMEM((4, 512, 2048), BF16),
            pltpu.VMEM((2, 2, 2, 3, 512, 256), BF16),
            pltpu.VMEM((2, 2, 2, 1, 512, 256), BF16),
            pltpu.VMEM((2, 4, 128), F32),
            pltpu.VMEM((3, 4, 128, 16, 128), BF16),
            pltpu.VMEM((2, 4, 8, 64, 256), BF16),
            pltpu.VMEM((4, 512, 2048), BF16),
            pltpu.VMEM((4, 2, 64, 2048), BF16),
            pltpu.VMEM((4, 2, 2, 64, 2048), BF16),
            pltpu.VMEM((4, 128, 2048), BF16),
            pltpu.SemaphoreType.DMA((SLOTS,)),
            pltpu.SemaphoreType.DMA((SLOTS,)),
        ],
        compiler_params=pltpu.CompilerParams(
            collective_id=0, has_side_effects=True, vmem_limit_bytes=60 * 1024 * 1024
        ),
    )(
        window_blocks.T,
        tok,
        norm_gain.reshape(1, width),
        qk_gain.reshape(2, 4, 128),
        w_spatial.transpose(1, 0, 2),
        w_temporal.transpose(1, 0, 2),
        w_out[:, 0, :].reshape(1, 128, 256),
        w_out[:, 1, :].reshape(1, 128, 256),
    )
    return res.reshape(2, 2, 64, width).transpose(0, 2, 1, 3).reshape(rows, frames, width)


def solution(mesh):
    return jax.shard_map(
        body,
        mesh=mesh,
        in_specs=(
            P("grp", "seq", None),
            P(),
            P(None, None, "grp", None),
            P(),
            P("seq", None, "grp"),
            P("seq", None, "grp"),
            P("seq", None, "grp"),
        ),
        out_specs=P("grp", "seq", None),
        check_vma=False,
    )
```

```python
import jax
import jax.numpy as jnp
from jax import lax
from jax.experimental import pallas as pl
from jax.experimental.pallas import tpu as pltpu
from jax.sharding import PartitionSpec as P

MESH = pl.DeviceIdType.MESH
EPS = 1e-06
F32 = jnp.float32
BF16 = jnp.bfloat16

TOK, WGT, OUTW, GAIN, RING_TL, RING_TR, RING_W, RING_O, RS, FIN = (
    0, 4, 6, 8, 10, 16, 22, 52, 82, 106,
)
SLOTS = 110


def mm(a, b):
    return jnp.dot(a, b, preferred_element_type=F32)


def mm_t(a, b):
    return lax.dot_general(a, b, (((1,), (1,)), ((), ())), preferred_element_type=F32)


def kernel(
    win, tok, norm_gain, gain, w_s, w_t, wo_s, wo_t, out,
    nrm, xs, wg, wo, gn, qkv, att, part, rs1, rs2, fin, snd, rcv,
):
    s, g = lax.axis_index("seq"), lax.axis_index("grp")
    c, y, xh = lax.rem(s, 2), lax.rem(lax.div(s, 2), 4), lax.div(s, 8)
    xl, z = lax.div(g, 4), lax.rem(g, 4)
    x = xh * 2 + xl
    nc = 1 - c
    unit = c * y + nc * z
    unit2 = nc * y + c * z
    local = nc * xl + c * xh

    def dev(xh_, y_, c_, xl_, z_):
        return ((xh_ * 4 + y_) * 2 + c_, xl_ * 4 + z_)

    def along(dy, dz):
        return dev(xh, lax.rem(y + dy, 4), c, xl, lax.rem(z + dz, 4))

    def across(dx):
        nx = lax.rem(x + dx, 4)
        return dev(lax.div(nx, 2), y, c, lax.rem(nx, 2), z)

    right, left = along(c, nc), along(3 * c, 3 * nc)
    right2, left2 = along(nc, c), along(3 * nc, 3 * c)
    right_x, left_x = across(1), across(3)

    barrier = pltpu.get_barrier_semaphore()
    peers = [right, left, right2, left2, right_x, left_x, dev(xh, y, nc, xl, z)]
    for b in range(2):
        peers.append(dev(xh, y, b, 1 - xl, z))
        peers.append(dev(1 - xh, y, b, xl, z))
        for a in range(2):
            peers.append(dev(xh, z, a, b, y))
    for to in peers:
        pl.semaphore_signal(barrier, inc=1, device_id=to, device_id_type=MESH)

    def remote(src, dst, i, j, to):
        return pltpu.make_async_remote_copy(
            src_ref=src, dst_ref=dst, send_sem=snd.at[i], recv_sem=rcv.at[j],
            device_id=to, device_id_type=MESH,
        )

    sends = []

    def put(src, dst, i, j, to):
        mine = jnp.logical_and(to[0] == s, to[1] == g)
        copy = remote(src, dst, i, j, to)

        @pl.when(mine)
        def _():
            pltpu.make_async_copy(src, dst, rcv.at[j]).start()

        @pl.when(jnp.logical_not(mine))
        def _():
            copy.start()

        sends.append((copy, jnp.logical_not(mine)))

    def arrived(dst, j):
        pltpu.make_async_copy(dst, dst, rcv.at[j]).wait()

    def start(copy):
        copy.start()
        sends.append((copy, None))

    class Ring:
        def __init__(self, view, at, to_right, to_left, base):
            self.view, self.base = view, base
            self.to = (to_right, to_left)
            self.units = (at, lax.rem(at + 3, 4), lax.rem(at + 1, 4), lax.rem(at + 2, 4))

        def send(self, u, half, k, side):
            ref = self.view(self.units[u], half)
            start(remote(ref, ref, self.base + k, self.base + k, self.to[side]))

        def wait(self, *slots):
            for k in slots:
                u, half = ((1, 0), (1, 1), (3, 0), (2, 1), (2, 0), (3, 1))[k]
                arrived(self.view(self.units[u], half), self.base + k)

        def begin(self):
            self.send(0, 0, 0, 0)
            self.send(0, 1, 3, 1)
            self.send(0, 1, 1, 0)
            self.send(0, 0, 4, 1)

        def forward(self):
            self.wait(0)
            self.send(1, 0, 2, 0)
            self.wait(3)
            self.send(2, 1, 5, 1)

        def forward_x(self):
            unit_ = (1 - xl) * self.units[2] + xl * self.units[1]
            to = tuple((1 - xl) * b + xl * a for a, b in zip(*self.to))
            for half, slot in ((0, 4 * (1 - xl)), (1, 3 - 2 * xl)):
                ref, k = self.view(unit_, half), self.base + 2 + 3 * half
                arrived(ref, self.base + slot)
                start(remote(ref, ref, k, k, to))

        def near_x(self):
            unit_ = (1 - xl) * self.units[1] + xl * self.units[2]
            for half, slot in ((0, 4 * xl), (1, 1 + 2 * xl)):
                arrived(self.view(unit_, half), self.base + slot)

    def token_ring(part_, base):
        return Ring(
            lambda u, h: xs.at[u, pl.ds((part_ * 2 + h) * 128, 128)], unit, right, left, base
        )

    def weight_rings(w, base):
        return (
            Ring(
                lambda u, h: w.at[xl, xh, 0, :, pl.ds(u * 128 + h * 64, 64)],
                unit2, right2, left2, base,
            ),
            Ring(
                lambda u, h: w.at[lax.rem(u, 2), lax.div(u, 2), 0, :, pl.ds(h * 256, 256)],
                x, right_x, left_x, base + 6,
            ),
            Ring(
                lambda u, h: w.at[
                    lax.rem(u, 2), lax.div(u, 2), 1, :, pl.ds(unit2 * 128 + h * 64, 64)
                ],
                x, right_x, left_x, base + 12,
            ),
            Ring(
                lambda u, h: w.at[1 - xl, h, 1, :, pl.ds(u * 128, 128)],
                unit2, right2, left2, base + 18,
            ),
            Ring(
                lambda u, h: w.at[xl, h, 1, :, pl.ds(u * 128, 128)],
                unit2, right2, left2, base + 24,
            ),
        )

    tok_l, tok_r = token_ring(local, RING_TL), token_ring(1 - local, RING_TR)
    w1a, w1b, w2a, w2b, w2c = weight_rings(wg, RING_W)
    o1a, o1b, o2a, o2b, o2c = weight_rings(wo, RING_O)

    def norm_half(h):
        def norm_rows(k, _):
            rows = pl.ds(pl.multiple_of(h * 128 + k * 32, 32), 32)
            v = tok[rows, :].astype(F32)
            scale = lax.rsqrt(jnp.mean(v * v, axis=-1, keepdims=True) + EPS)
            v = (v * scale * norm_gain[...]).astype(BF16)
            for old in range(16):
                new = (old // 8 * 2 + old % 2) * 4 + old // 2 % 4
                nrm[rows, new * 128 : new * 128 + 128] = v[:, old * 128 : old * 128 + 128]
            return 0

        lax.fori_loop(0, 4, norm_rows, 0)

    norm_half(0)
    norm_half(1)
    pl.semaphore_wait(barrier, len(peers))

    to_s, to_t = dev(xh, y, 0, xl, z), dev(xh, z, 1, xl, y)
    mine_w, mine_o = (w.at[xl, xh, c, :, pl.ds(y * 128, 128)] for w in (wg, wo))
    put(w_s, mine_w, WGT, WGT + c, to_s)
    put(w_t, mine_w, WGT + 1, WGT + c, to_t)
    for h in range(2):
        src = nrm.at[pl.ds(h * 128, 128)]
        i_s, i_t = xl * 2 + h, xh * 2 + c
        put(src, xs.at[z, pl.ds(i_s * 128, 128)], TOK + h, TOK + i_s, dev(xh, y, 0, c, z))
        put(src, xs.at[y, pl.ds(i_t * 128, 128)], TOK + 2 + h, TOK + i_t, dev(h, y, 1, xl, z))
    put(wo_s, mine_o, OUTW, OUTW + c, to_s)
    put(wo_t, mine_o, OUTW + 1, OUTW + c, to_t)
    for h in range(2):
        put(
            gain.at[c], gn.at[xl], GAIN + h, GAIN + xl,
            dev(xh, nc * y + c * z, c, h, nc * z + c * y),
        )

    def rows_arrived(w, i, slot):
        arrived(w.at[xl, xh, i, :, pl.ds(unit2 * 128, 128)], slot + i)

    def tokens_arrived(half):
        for h in range(2):
            i = half * 2 + h
            arrived(xs.at[unit, pl.ds(i * 128, 128)], TOK + i)

    tokens_arrived(local)
    tok_l.begin()
    rows_arrived(wg, 0, WGT)
    w1a.begin()
    rows_arrived(wg, 1, WGT)
    w2a.begin()
    tok_l.forward()
    w1a.forward()
    tokens_arrived(1 - local)
    tok_r.begin()
    w2a.forward()
    for i in range(2):
        rows_arrived(wo, i, OUTW)
    o1a.begin()
    o2a.begin()
    w1a.wait(1, 4, 2, 5)
    w1b.begin()
    w2a.wait(1, 4, 2, 5)
    w2b.begin()
    tok_r.forward()
    o1a.forward()
    o2a.forward()
    w2b.forward()
    w1b.forward_x()
    w2c.begin()
    tok_l.wait(1, 4, 2, 5)
    for i in range(2):
        arrived(gn.at[i], GAIN + i)
    tok_r.wait(1, 4, 2, 5)
    w1b.near_x()
    w2b.wait(1, 4, 2, 5)

    def project(pair, first, last):
        def one(u, _):
            w = [wg[pair, :, :, n].reshape(2048, 256) for n in range(3)]
            acc = mm(xs[u], jnp.concatenate(w, axis=1))
            for n in range(3):
                for j in range(2):
                    a = acc[:, n * 256 + j * 128 : n * 256 + j * 128 + 128]
                    if n < 2:
                        a = a * lax.rsqrt(jnp.mean(a * a, axis=-1, keepdims=True) + EPS)
                        a = a * gn[pair, 2 * n + j : 2 * n + j + 1, :]
                    if n == 0:
                        a = a * (128 ** -0.5)

                    @pl.when(c == 0)
                    def _():
                        b = a.astype(BF16)
                        for k in range(8):
                            i, f = k // 2, k % 2
                            first = f * 64 + ((i // 2) * 4 + u) * 8 + i % 2 * 4
                            qkv[n, pair * 2 + j, pl.ds(first, 4)] = b[
                                k * 64 : k * 64 + 64
                            ].reshape(4, 16, 128)

                    @pl.when(c == 1)
                    def _():
                        for i in range(4):
                            for m in range(8):
                                at = i * 128 + m * 8
                                b = jnp.concatenate([a[at : at + 8], a[at + 64 : at + 72]], axis=0)
                                at = m * 16 + ((i // 2) * 4 + u) * 2 + i % 2
                                qkv[n, pair * 2 + j, at] = b.astype(BF16)
            return 0

        lax.fori_loop(first, last, one, 0)

    def softmax_mix(sc, v):
        e = jnp.exp(sc - jnp.max(sc, axis=-1, keepdims=True)).astype(BF16)
        o = mm(e, jnp.concatenate([v, jnp.ones_like(v)], axis=1))
        return o[:, 0:128] / o[:, 128:256]

    def tile(n, hd, first, rows=128):
        return qkv[n, hd, pl.ds(first, rows // 16)].reshape(rows, 128)

    def attend(pair, half):
        @pl.when(c == 0)
        def _():
            def spatial(k, _):
                t = half * 4 + k
                for f in range(2):
                    at = [f * 64 + win[j, t] * 8 for j in range(4)]
                    for j in range(2):
                        hd = pair * 2 + j
                        q = tile(0, hd, f * 64 + t * 8)
                        keys = jnp.concatenate([tile(1, hd, a) for a in at], axis=0)
                        vals = jnp.concatenate([tile(2, hd, a) for a in at], axis=0)
                        o = softmax_mix(mm_t(q, keys), vals).astype(BF16)
                        for h in range(2):
                            att[
                                pair, k, half * 4 + h * 2 + f, :, j * 128 : j * 128 + 128
                            ] = o[h * 64 : h * 64 + 64]
                return 0

            lax.fori_loop(0, 4, spatial, 0)

        for b in range(2):
            @pl.when(jnp.logical_and(c == 1, half == b))
            def _():
                def temporal(pg, _):
                    rows = pl.ds(pl.multiple_of(pg * 16, 16), 16)
                    keys = 128 * (b + 1)
                    qi = lax.broadcasted_iota(jnp.int32, (128, keys), 0) + b * 128
                    ki = lax.broadcasted_iota(jnp.int32, (128, keys), 1)
                    ok = jnp.logical_and(
                        jnp.bitwise_and(qi, 7) == jnp.bitwise_and(ki, 7), ki <= qi
                    )
                    for j in range(2):
                        hd = pair * 2 + j
                        res = []
                        for m in range(2):
                            first = pg * 32 + m * 16
                            q = tile(0, hd, first + b * 8)
                            sc = mm_t(q, tile(1, hd, first, keys))
                            res.append(
                                softmax_mix(jnp.where(ok, sc, -1e30), tile(2, hd, first, keys))
                            )
                        for m in range(16):
                            fr = b * 16 + m
                            i = b * 2 + (fr // 2) % 2
                            o = jnp.concatenate([v[m * 8 : m * 8 + 8] for v in res], axis=0)
                            att[
                                pair, fr // 4 % 4, i * 2 + fr % 2, rows, j * 128 : j * 128 + 128
                            ] = o.astype(BF16)
                    return 0

                lax.fori_loop(0, 4, temporal, 0)

    project(1 - xl, 0, 2)
    w2c.forward()
    o1a.wait(1, 4, 2, 5)
    o1b.begin()
    o2a.wait(1, 4, 2, 5)
    o2b.begin()
    o2c.begin()
    project(1 - xl, 2, 4)
    attend(1 - xl, 0)
    o1b.forward_x()
    o2b.forward()
    o2c.forward()
    attend(1 - xl, 1)
    w1b.wait(2, 5)
    w2c.wait(1, 4, 2, 5)
    project(xl, 0, 2)
    project(xl, 2, 4)
    attend(xl, 1 - local)
    o1b.near_x()
    o1b.wait(2, 5)
    o2b.wait(1, 4, 2, 5)
    o2c.wait(1, 4, 2, 5)

    def outproj(u, half):
        def one(k, _):
            rows = pl.ds(pl.multiple_of(half * 256, 256), 256)
            o = [att[p, u, pl.ds(half * 4, 4)].reshape(256, 256) for p in range(2)]
            for b in range(2):
                acc = mm_t(o[0], wo[0, k, b, 0]) + mm_t(o[1], wo[1, k, b, 0])
                for q in range(4):
                    cols = pl.ds(pl.multiple_of(k * 1024 + q * 256 + b * 128, 128), 128)
                    part[u, rows, cols] = acc[:, q * 128 : q * 128 + 128].astype(BF16)
            return 0

        lax.fori_loop(0, 2, one, 0)

    def add_rows(u, first, *others):
        def one(k, _):
            rows = pl.ds(pl.multiple_of(first + k * 32, 32), 32)
            here = pl.ds(pl.multiple_of(k * 32, 32), 32)
            total = part[u, rows, :].astype(F32)
            for other in others:
                total = total + other[here, :].astype(F32)
            part[u, rows, :] = total.astype(BF16)
            return 0

        lax.fori_loop(0, 2, one, 0)

    u_l, u_r, u_2 = lax.rem(unit + 3, 4), lax.rem(unit + 1, 4), lax.rem(unit + 2, 4)
    pieces = [(1 - local) * 2, (1 - local) * 2 + 1, local * 2, local * 2 + 1]

    def reduce_send(n, u, q, dst, k, to):
        src = part.at[u, pl.ds(pieces[n] * 128 + q * 64, 64)]
        start(remote(src, dst, RS + n * 6 + k, RS + n * 6 + k, to))

    def reduce_start(half, n):
        outproj(u_2, half)
        reduce_send(n, u_2, 0, rs1.at[n, 0], 0, right)
        reduce_send(n, u_2, 1, rs1.at[n, 1], 1, left)
        outproj(u_r, half)
        reduce_send(n, u_r, 1, rs2.at[n, 0, 1], 2, right)
        outproj(u_l, half)
        reduce_send(n, u_l, 0, rs2.at[n, 1, 0], 3, left)
        reduce_send(n + 1, u_2, 0, rs1.at[n + 1, 0], 0, right)
        reduce_send(n + 1, u_2, 1, rs1.at[n + 1, 1], 1, left)
        reduce_send(n + 1, u_r, 1, rs2.at[n + 1, 0, 1], 2, right)
        reduce_send(n + 1, u_l, 0, rs2.at[n + 1, 1, 0], 3, left)

    def reduce_pass(n):
        arrived(rs1.at[n, 0], RS + n * 6)
        add_rows(u_r, pieces[n] * 128, rs1.at[n, 0])
        reduce_send(n, u_r, 0, rs2.at[n, 0, 0], 4, right)
        arrived(rs1.at[n, 1], RS + n * 6 + 1)
        add_rows(u_l, pieces[n] * 128 + 64, rs1.at[n, 1])
        reduce_send(n, u_l, 1, rs2.at[n, 1, 1], 5, left)

    def reduce_end(half, n):
        h = n % 2
        for q in range(2):
            arrived(rs2.at[n, 1 - q, q], RS + n * 6 + 3 - q)
            arrived(rs2.at[n, q, q], RS + n * 6 + 4 + q)
            add_rows(unit, pieces[n] * 128 + q * 64, rs2.at[n, 0, q], rs2.at[n, 1, q])
        at = nc * h + c * (2 + xh)
        to = dev(nc * xh + c * half, y, nc * xl + c * h, nc * half + c * xl, z)
        put(part.at[unit, pl.ds(pieces[n] * 128, 128)], fin.at[at], FIN + n, FIN + at, to)

    reduce_start(1 - local, 0)
    attend(xl, local)
    reduce_pass(0)
    reduce_pass(1)
    outproj(unit, 1 - local)
    reduce_start(local, 2)
    reduce_end(1 - local, 0)
    reduce_end(1 - local, 1)
    reduce_pass(2)
    reduce_pass(3)
    outproj(unit, local)
    reduce_end(local, 2)
    reduce_end(local, 3)

    for h in range(2):
        arrived(fin.at[h], FIN + h)
        arrived(fin.at[2 + h], FIN + 2 + h)

        def total_rows(k, _):
            rows = pl.ds(pl.multiple_of(k * 32, 32), 32)
            here = pl.ds(pl.multiple_of(h * 128 + k * 32, 32), 32)
            total = fin[h, rows, :].astype(F32) + fin[2 + h, rows, :].astype(F32)
            out[here, :] = (tok[here, :].astype(F32) + total).astype(BF16)
            return 0

        lax.fori_loop(0, 4, total_rows, 0)

    for copy, cond in sends:
        if cond is None:
            copy.wait_send()
        else:
            pl.when(cond)(copy.wait_send)


def body(tokens, norm_gain, qk_gain, window_blocks, w_spatial, w_temporal, w_out):
    rows, frames, width = tokens.shape
    tok = tokens.reshape(2, 64, 2, width).transpose(0, 2, 1, 3).reshape(256, width)
    vmem = pl.BlockSpec(memory_space=pltpu.VMEM)
    res = pl.pallas_call(
        kernel,
        name="attention_block",
        out_shape=jax.ShapeDtypeStruct((256, width), BF16),
        in_specs=[pl.BlockSpec(memory_space=pltpu.SMEM)] + [vmem] * 7,
        out_specs=vmem,
        scratch_shapes=[
            pltpu.VMEM((256, 2048), BF16),
            pltpu.VMEM((4, 512, 2048), BF16),
            pltpu.VMEM((2, 2, 2, 3, 512, 256), BF16),
            pltpu.VMEM((2, 2, 2, 1, 512, 256), BF16),
            pltpu.VMEM((2, 4, 128), F32),
            pltpu.VMEM((3, 4, 128, 16, 128), BF16),
            pltpu.VMEM((2, 4, 8, 64, 256), BF16),
            pltpu.VMEM((4, 512, 2048), BF16),
            pltpu.VMEM((4, 2, 64, 2048), BF16),
            pltpu.VMEM((4, 2, 2, 64, 2048), BF16),
            pltpu.VMEM((4, 128, 2048), BF16),
            pltpu.SemaphoreType.DMA((SLOTS,)),
            pltpu.SemaphoreType.DMA((SLOTS,)),
        ],
        compiler_params=pltpu.CompilerParams(
            collective_id=0, has_side_effects=True, vmem_limit_bytes=60 * 1024 * 1024
        ),
    )(
        window_blocks.T,
        tok,
        norm_gain.reshape(1, width),
        qk_gain.reshape(2, 4, 128),
        w_spatial.transpose(1, 0, 2),
        w_temporal.transpose(1, 0, 2),
        w_out[:, 0, :].reshape(1, 128, 256),
        w_out[:, 1, :].reshape(1, 128, 256),
    )
    return res.reshape(2, 2, 64, width).transpose(0, 2, 1, 3).reshape(rows, frames, width)


def solution(mesh):
    return jax.shard_map(
        body,
        mesh=mesh,
        in_specs=(
            P("grp", "seq", None),
            P(),
            P(None, None, "grp", None),
            P(),
            P("seq", None, "grp"),
            P("seq", None, "grp"),
            P("seq", None, "grp"),
        ),
        out_specs=P("grp", "seq", None),
        check_vma=False,
    )
```

```python
import jax
import jax.numpy as jnp
from jax import lax
from jax.experimental import pallas as pl
from jax.experimental.pallas import tpu as pltpu
from jax.sharding import PartitionSpec as P

MESH = pl.DeviceIdType.MESH
EPS = 1e-06
F32 = jnp.float32
BF16 = jnp.bfloat16

TOK, WGT, OUTW, GAIN, RING_TL, RING_TR, RING_W, RING_O, RS, FIN = (
    0, 4, 6, 8, 10, 16, 22, 52, 82, 106,
)
SLOTS = 110


def mm(a, b):
    return jnp.dot(a, b, preferred_element_type=F32)


def mm_t(a, b):
    return lax.dot_general(a, b, (((1,), (1,)), ((), ())), preferred_element_type=F32)


def kernel(
    win, tok, norm_gain, gain, w_s, w_t, w_o, out,
    nrm, wo_own, xs, wg, wo, gn, qkv, att, part, rs1, rs2, fin, snd, rcv,
):
    s, g = lax.axis_index("seq"), lax.axis_index("grp")
    c, y, xh = lax.rem(s, 2), lax.rem(lax.div(s, 2), 4), lax.div(s, 8)
    xl, z = lax.div(g, 4), lax.rem(g, 4)
    x = xh * 2 + xl
    nc = 1 - c
    unit = c * y + nc * z
    unit2 = nc * y + c * z
    local = nc * xl + c * xh

    def dev(xh_, y_, c_, xl_, z_):
        return ((xh_ * 4 + y_) * 2 + c_, xl_ * 4 + z_)

    def along(dy, dz):
        return dev(xh, lax.rem(y + dy, 4), c, xl, lax.rem(z + dz, 4))

    def across(dx):
        nx = lax.rem(x + dx, 4)
        return dev(lax.div(nx, 2), y, c, lax.rem(nx, 2), z)

    right, left = along(c, nc), along(3 * c, 3 * nc)
    right2, left2 = along(nc, c), along(3 * nc, 3 * c)
    right_x, left_x = across(1), across(3)

    barrier = pltpu.get_barrier_semaphore()
    peers = [right, left, right2, left2, right_x, left_x, dev(xh, y, nc, xl, z)]
    for b in range(2):
        peers.append(dev(xh, y, b, 1 - xl, z))
        peers.append(dev(1 - xh, y, b, xl, z))
        for a in range(2):
            peers.append(dev(xh, z, a, b, y))
    for to in peers:
        pl.semaphore_signal(barrier, inc=1, device_id=to, device_id_type=MESH)

    def remote(src, dst, i, j, to):
        return pltpu.make_async_remote_copy(
            src_ref=src, dst_ref=dst, send_sem=snd.at[i], recv_sem=rcv.at[j],
            device_id=to, device_id_type=MESH,
        )

    sends = []

    def put(src, dst, i, j, to):
        mine = jnp.logical_and(to[0] == s, to[1] == g)
        copy = remote(src, dst, i, j, to)

        @pl.when(mine)
        def _():
            pltpu.make_async_copy(src, dst, rcv.at[j]).start()

        @pl.when(jnp.logical_not(mine))
        def _():
            copy.start()

        sends.append((copy, jnp.logical_not(mine)))

    def arrived(dst, j):
        pltpu.make_async_copy(dst, dst, rcv.at[j]).wait()

    def start(copy):
        copy.start()
        sends.append((copy, None))

    class Ring:
        def __init__(self, view, at, to_right, to_left, base):
            self.view, self.base = view, base
            self.to = (to_right, to_left)
            self.units = (at, lax.rem(at + 3, 4), lax.rem(at + 1, 4), lax.rem(at + 2, 4))

        def send(self, u, half, k, side):
            ref = self.view(self.units[u], half)
            start(remote(ref, ref, self.base + k, self.base + k, self.to[side]))

        def wait(self, *slots):
            for k in slots:
                u, half = ((1, 0), (1, 1), (3, 0), (2, 1), (2, 0), (3, 1))[k]
                arrived(self.view(self.units[u], half), self.base + k)

        def begin(self):
            self.send(0, 0, 0, 0)
            self.send(0, 1, 3, 1)
            self.send(0, 1, 1, 0)
            self.send(0, 0, 4, 1)

        def forward(self):
            self.wait(0)
            self.send(1, 0, 2, 0)
            self.wait(3)
            self.send(2, 1, 5, 1)

        def forward_x(self):
            unit_ = (1 - xl) * self.units[2] + xl * self.units[1]
            to = tuple((1 - xl) * b + xl * a for a, b in zip(*self.to))
            for half, slot in ((0, 4 * (1 - xl)), (1, 3 - 2 * xl)):
                ref, k = self.view(unit_, half), self.base + 2 + 3 * half
                arrived(ref, self.base + slot)
                start(remote(ref, ref, k, k, to))

        def near_x(self):
            unit_ = (1 - xl) * self.units[1] + xl * self.units[2]
            for half, slot in ((0, 4 * xl), (1, 1 + 2 * xl)):
                arrived(self.view(unit_, half), self.base + slot)

    def token_ring(part_, base):
        return Ring(
            lambda u, h: xs.at[u, pl.ds((part_ * 2 + h) * 128, 128)], unit, right, left, base
        )

    def weight_rings(w, base):
        return (
            Ring(
                lambda u, h: w.at[xl, xh, 0, :, pl.ds(u * 128 + h * 64, 64)],
                unit2, right2, left2, base,
            ),
            Ring(
                lambda u, h: w.at[lax.rem(u, 2), lax.div(u, 2), 0, :, pl.ds(h * 256, 256)],
                x, right_x, left_x, base + 6,
            ),
            Ring(
                lambda u, h: w.at[
                    lax.rem(u, 2), lax.div(u, 2), 1, :, pl.ds(unit2 * 128 + h * 64, 64)
                ],
                x, right_x, left_x, base + 12,
            ),
            Ring(
                lambda u, h: w.at[1 - xl, h, 1, :, pl.ds(u * 128, 128)],
                unit2, right2, left2, base + 18,
            ),
            Ring(
                lambda u, h: w.at[xl, h, 1, :, pl.ds(u * 128, 128)],
                unit2, right2, left2, base + 24,
            ),
        )

    tok_l, tok_r = token_ring(local, RING_TL), token_ring(1 - local, RING_TR)
    w1a, w1b, w2a, w2b, w2c = weight_rings(wg, RING_W)
    o1a, o1b, o2a, o2b, o2c = weight_rings(wo, RING_O)

    def norm_half(h):
        def norm_rows(k, _):
            rows = pl.ds(pl.multiple_of(h * 128 + k * 32, 32), 32)
            v = tok[rows, :].astype(F32)
            scale = lax.rsqrt(jnp.mean(v * v, axis=-1, keepdims=True) + EPS)
            v = (v * scale * norm_gain[...]).astype(BF16)
            for old in range(16):
                new = (old // 8 * 2 + old % 2) * 4 + old // 2 % 4
                nrm[rows, new * 128 : new * 128 + 128] = v[:, old * 128 : old * 128 + 128]
            return 0

        lax.fori_loop(0, 4, norm_rows, 0)

    norm_half(0)
    norm_half(1)
    pl.semaphore_wait(barrier, len(peers))

    to_s, to_t = dev(xh, y, 0, xl, z), dev(xh, z, 1, xl, y)
    mine_w, mine_o = (w.at[xl, xh, c, :, pl.ds(y * 128, 128)] for w in (wg, wo))
    put(w_s, mine_w, WGT, WGT + c, to_s)
    put(w_t, mine_w, WGT + 1, WGT + c, to_t)
    for h in range(2):
        src = nrm.at[pl.ds(h * 128, 128)]
        i_s, i_t = xl * 2 + h, xh * 2 + c
        put(src, xs.at[z, pl.ds(i_s * 128, 128)], TOK + h, TOK + i_s, dev(xh, y, 0, c, z))
        put(src, xs.at[y, pl.ds(i_t * 128, 128)], TOK + 2 + h, TOK + i_t, dev(h, y, 1, xl, z))
    for b in range(2):
        wo_own[b, 0] = w_o[...].astype(F32)[:, b, :].astype(BF16)
    put(wo_own.at[0], mine_o, OUTW, OUTW + c, to_s)
    put(wo_own.at[1], mine_o, OUTW + 1, OUTW + c, to_t)
    for h in range(2):
        put(
            gain.at[c], gn.at[xl], GAIN + h, GAIN + xl,
            dev(xh, nc * y + c * z, c, h, nc * z + c * y),
        )

    def rows_arrived(w, i, slot):
        arrived(w.at[xl, xh, i, :, pl.ds(unit2 * 128, 128)], slot + i)

    def tokens_arrived(half):
        for h in range(2):
            i = half * 2 + h
            arrived(xs.at[unit, pl.ds(i * 128, 128)], TOK + i)

    tokens_arrived(local)
    tok_l.begin()
    rows_arrived(wg, 0, WGT)
    w1a.begin()
    rows_arrived(wg, 1, WGT)
    w2a.begin()
    tok_l.forward()
    w1a.forward()
    tokens_arrived(1 - local)
    tok_r.begin()
    w2a.forward()
    for i in range(2):
        rows_arrived(wo, i, OUTW)
    o1a.begin()
    o2a.begin()
    w1a.wait(1, 4, 2, 5)
    w1b.begin()
    w2a.wait(1, 4, 2, 5)
    w2b.begin()
    tok_r.forward()
    o1a.forward()
    o2a.forward()
    w2b.forward()
    w1b.forward_x()
    w2c.begin()
    tok_l.wait(1, 4, 2, 5)
    for i in range(2):
        arrived(gn.at[i], GAIN + i)
    tok_r.wait(1, 4, 2, 5)
    w1b.near_x()
    w2b.wait(1, 4, 2, 5)

    def project(pair, first, last):
        def one(u, _):
            w = [wg[pair, :, :, n].reshape(2048, 256) for n in range(3)]
            acc = mm(xs[u], jnp.concatenate(w, axis=1))
            for n in range(3):
                for j in range(2):
                    a = acc[:, n * 256 + j * 128 : n * 256 + j * 128 + 128]
                    if n < 2:
                        a = a * lax.rsqrt(jnp.mean(a * a, axis=-1, keepdims=True) + EPS)
                        a = a * gn[pair, 2 * n + j : 2 * n + j + 1, :]
                    if n == 0:
                        a = a * (128 ** -0.5)

                    @pl.when(c == 0)
                    def _():
                        b = a.astype(BF16)
                        for k in range(8):
                            i, f = k // 2, k % 2
                            first = f * 64 + ((i // 2) * 4 + u) * 8 + i % 2 * 4
                            qkv[n, pair * 2 + j, pl.ds(first, 4)] = b[
                                k * 64 : k * 64 + 64
                            ].reshape(4, 16, 128)

                    @pl.when(c == 1)
                    def _():
                        for i in range(4):
                            for m in range(8):
                                at = i * 128 + m * 8
                                b = jnp.concatenate([a[at : at + 8], a[at + 64 : at + 72]], axis=0)
                                at = m * 16 + ((i // 2) * 4 + u) * 2 + i % 2
                                qkv[n, pair * 2 + j, at] = b.astype(BF16)
            return 0

        lax.fori_loop(first, last, one, 0)

    def softmax_mix(sc, v):
        e = jnp.exp(sc - jnp.max(sc, axis=-1, keepdims=True)).astype(BF16)
        o = mm(e, jnp.concatenate([v, jnp.ones_like(v)], axis=1))
        return o[:, 0:128] / o[:, 128:256]

    def tile(n, hd, first, rows=128):
        return qkv[n, hd, pl.ds(first, rows // 16)].reshape(rows, 128)

    def attend(pair, half):
        @pl.when(c == 0)
        def _():
            def spatial(k, _):
                t = half * 4 + k
                for f in range(2):
                    at = [f * 64 + win[j, t] * 8 for j in range(4)]
                    for j in range(2):
                        hd = pair * 2 + j
                        q = tile(0, hd, f * 64 + t * 8)
                        keys = jnp.concatenate([tile(1, hd, a) for a in at], axis=0)
                        vals = jnp.concatenate([tile(2, hd, a) for a in at], axis=0)
                        o = softmax_mix(mm_t(q, keys), vals).astype(BF16)
                        for h in range(2):
                            att[
                                pair, k, half * 4 + h * 2 + f, :, j * 128 : j * 128 + 128
                            ] = o[h * 64 : h * 64 + 64]
                return 0

            lax.fori_loop(0, 4, spatial, 0)

        for b in range(2):
            @pl.when(jnp.logical_and(c == 1, half == b))
            def _():
                def temporal(pg, _):
                    rows = pl.ds(pl.multiple_of(pg * 16, 16), 16)
                    keys = 128 * (b + 1)
                    qi = lax.broadcasted_iota(jnp.int32, (128, keys), 0) + b * 128
                    ki = lax.broadcasted_iota(jnp.int32, (128, keys), 1)
                    ok = jnp.logical_and(
                        jnp.bitwise_and(qi, 7) == jnp.bitwise_and(ki, 7), ki <= qi
                    )
                    for j in range(2):
                        hd = pair * 2 + j
                        res = []
                        for m in range(2):
                            first = pg * 32 + m * 16
                            q = tile(0, hd, first + b * 8)
                            sc = mm_t(q, tile(1, hd, first, keys))
                            res.append(
                                softmax_mix(jnp.where(ok, sc, -1e30), tile(2, hd, first, keys))
                            )
                        for m in range(16):
                            fr = b * 16 + m
                            i = b * 2 + (fr // 2) % 2
                            o = jnp.concatenate([v[m * 8 : m * 8 + 8] for v in res], axis=0)
                            att[
                                pair, fr // 4 % 4, i * 2 + fr % 2, rows, j * 128 : j * 128 + 128
                            ] = o.astype(BF16)
                    return 0

                lax.fori_loop(0, 4, temporal, 0)

    project(1 - xl, 0, 2)
    w2c.forward()
    o1a.wait(1, 4, 2, 5)
    o1b.begin()
    o2a.wait(1, 4, 2, 5)
    o2b.begin()
    o2c.begin()
    project(1 - xl, 2, 4)
    attend(1 - xl, 0)
    o1b.forward_x()
    o2b.forward()
    o2c.forward()
    attend(1 - xl, 1)
    w1b.wait(2, 5)
    w2c.wait(1, 4, 2, 5)
    project(xl, 0, 2)
    project(xl, 2, 4)
    attend(xl, 1 - local)
    o1b.near_x()
    o1b.wait(2, 5)
    o2b.wait(1, 4, 2, 5)
    o2c.wait(1, 4, 2, 5)

    def outproj(u, half):
        def one(k, _):
            rows = pl.ds(pl.multiple_of(half * 256, 256), 256)
            o = [att[p, u, pl.ds(half * 4, 4)].reshape(256, 256) for p in range(2)]
            for b in range(2):
                acc = mm_t(o[0], wo[0, k, b, 0]) + mm_t(o[1], wo[1, k, b, 0])
                for q in range(4):
                    cols = pl.ds(pl.multiple_of(k * 1024 + q * 256 + b * 128, 128), 128)
                    part[u, rows, cols] = acc[:, q * 128 : q * 128 + 128].astype(BF16)
            return 0

        lax.fori_loop(0, 2, one, 0)

    def add_rows(u, first, *others):
        def one(k, _):
            rows = pl.ds(pl.multiple_of(first + k * 32, 32), 32)
            here = pl.ds(pl.multiple_of(k * 32, 32), 32)
            total = part[u, rows, :].astype(F32)
            for other in others:
                total = total + other[here, :].astype(F32)
            part[u, rows, :] = total.astype(BF16)
            return 0

        lax.fori_loop(0, 2, one, 0)

    u_l, u_r, u_2 = lax.rem(unit + 3, 4), lax.rem(unit + 1, 4), lax.rem(unit + 2, 4)
    pieces = [(1 - local) * 2, (1 - local) * 2 + 1, local * 2, local * 2 + 1]

    def reduce_send(n, u, q, dst, k, to):
        src = part.at[u, pl.ds(pieces[n] * 128 + q * 64, 64)]
        start(remote(src, dst, RS + n * 6 + k, RS + n * 6 + k, to))

    def reduce_start(half, n):
        outproj(u_2, half)
        reduce_send(n, u_2, 0, rs1.at[n, 0], 0, right)
        reduce_send(n, u_2, 1, rs1.at[n, 1], 1, left)
        outproj(u_r, half)
        reduce_send(n, u_r, 1, rs2.at[n, 0, 1], 2, right)
        outproj(u_l, half)
        reduce_send(n, u_l, 0, rs2.at[n, 1, 0], 3, left)
        reduce_send(n + 1, u_2, 0, rs1.at[n + 1, 0], 0, right)
        reduce_send(n + 1, u_2, 1, rs1.at[n + 1, 1], 1, left)
        reduce_send(n + 1, u_r, 1, rs2.at[n + 1, 0, 1], 2, right)
        reduce_send(n + 1, u_l, 0, rs2.at[n + 1, 1, 0], 3, left)

    def reduce_pass(n):
        arrived(rs1.at[n, 0], RS + n * 6)
        add_rows(u_r, pieces[n] * 128, rs1.at[n, 0])
        reduce_send(n, u_r, 0, rs2.at[n, 0, 0], 4, right)
        arrived(rs1.at[n, 1], RS + n * 6 + 1)
        add_rows(u_l, pieces[n] * 128 + 64, rs1.at[n, 1])
        reduce_send(n, u_l, 1, rs2.at[n, 1, 1], 5, left)

    def reduce_end(half, n):
        h = n % 2
        for q in range(2):
            arrived(rs2.at[n, 1 - q, q], RS + n * 6 + 3 - q)
            arrived(rs2.at[n, q, q], RS + n * 6 + 4 + q)
            add_rows(unit, pieces[n] * 128 + q * 64, rs2.at[n, 0, q], rs2.at[n, 1, q])
        at = nc * h + c * (2 + xh)
        to = dev(nc * xh + c * half, y, nc * xl + c * h, nc * half + c * xl, z)
        put(part.at[unit, pl.ds(pieces[n] * 128, 128)], fin.at[at], FIN + n, FIN + at, to)

    reduce_start(1 - local, 0)
    attend(xl, local)
    reduce_pass(0)
    reduce_pass(1)
    outproj(unit, 1 - local)
    reduce_start(local, 2)
    reduce_end(1 - local, 0)
    reduce_end(1 - local, 1)
    reduce_pass(2)
    reduce_pass(3)
    outproj(unit, local)
    reduce_end(local, 2)
    reduce_end(local, 3)

    for h in range(2):
        arrived(fin.at[h], FIN + h)
        arrived(fin.at[2 + h], FIN + 2 + h)

        def total_rows(k, _):
            rows = pl.ds(pl.multiple_of(k * 32, 32), 32)
            here = pl.ds(pl.multiple_of(h * 128 + k * 32, 32), 32)
            total = fin[h, rows, :].astype(F32) + fin[2 + h, rows, :].astype(F32)
            out[here, :] = (tok[here, :].astype(F32) + total).astype(BF16)
            return 0

        lax.fori_loop(0, 4, total_rows, 0)

    for copy, cond in sends:
        if cond is None:
            copy.wait_send()
        else:
            pl.when(cond)(copy.wait_send)


def body(tokens, norm_gain, qk_gain, window_blocks, w_spatial, w_temporal, w_out):
    rows, frames, width = tokens.shape
    tok = tokens.reshape(2, 64, 2, width).transpose(0, 2, 1, 3).reshape(256, width)
    vmem = pl.BlockSpec(memory_space=pltpu.VMEM)
    res = pl.pallas_call(
        kernel,
        name="attention_block",
        out_shape=pltpu.VMEM((256, width), BF16),
        in_specs=[pl.BlockSpec(memory_space=pltpu.SMEM)] + [vmem] * 6,
        out_specs=vmem,
        scratch_shapes=[
            pltpu.VMEM((256, 2048), BF16),
            pltpu.VMEM((2, 1, 128, 256), BF16),
            pltpu.VMEM((4, 512, 2048), BF16),
            pltpu.VMEM((2, 2, 2, 3, 512, 256), BF16),
            pltpu.VMEM((2, 2, 2, 1, 512, 256), BF16),
            pltpu.VMEM((2, 4, 128), F32),
            pltpu.VMEM((3, 4, 128, 16, 128), BF16),
            pltpu.VMEM((2, 4, 8, 64, 256), BF16),
            pltpu.VMEM((4, 512, 2048), BF16),
            pltpu.VMEM((4, 2, 64, 2048), BF16),
            pltpu.VMEM((4, 2, 2, 64, 2048), BF16),
            pltpu.VMEM((4, 128, 2048), BF16),
            pltpu.SemaphoreType.DMA((SLOTS,)),
            pltpu.SemaphoreType.DMA((SLOTS,)),
        ],
        compiler_params=pltpu.CompilerParams(
            collective_id=0, has_side_effects=True, vmem_limit_bytes=60 * 1024 * 1024
        ),
    )(
        window_blocks.T,
        pltpu.with_memory_space_constraint(tok, pltpu.VMEM),
        norm_gain.reshape(1, width),
        qk_gain.reshape(2, 4, 128),
        w_spatial.transpose(1, 0, 2),
        w_temporal.transpose(1, 0, 2),
        w_out,
    )
    return res.reshape(2, 2, 64, width).transpose(0, 2, 1, 3).reshape(rows, frames, width)


def solution(mesh):
    return jax.shard_map(
        body,
        mesh=mesh,
        in_specs=(
            P("grp", "seq", None),
            P(),
            P(None, None, "grp", None),
            P(),
            P("seq", None, "grp"),
            P("seq", None, "grp"),
            P("seq", None, "grp"),
        ),
        out_specs=P("grp", "seq", None),
        check_vma=False,
    )
```

```python
import jax
import jax.numpy as jnp
from jax import lax
from jax.experimental import pallas as pl
from jax.experimental.pallas import tpu as pltpu
from jax.sharding import PartitionSpec as P

MESH = pl.DeviceIdType.MESH
EPS = 1e-06
F32 = jnp.float32
BF16 = jnp.bfloat16

TOK, WGT, OUTW, GAIN, RING_TL, RING_TR, RING_W, RING_O, RS, FIN = (
    0, 4, 6, 8, 10, 16, 22, 52, 82, 106,
)
SLOTS = 110


def mm(a, b):
    return jnp.dot(a, b, preferred_element_type=F32)


def mm_t(a, b):
    return lax.dot_general(a, b, (((1,), (1,)), ((), ())), preferred_element_type=F32)


def kernel(
    win, tok, norm_gain, gain, w_s, w_t, w_o, out,
    nrm, wo_own, xs, wg, wo, gn, qkv, att, part, rs1, rs2, fin, snd, rcv,
):
    s, g = lax.axis_index("seq"), lax.axis_index("grp")
    c, y, xh = lax.rem(s, 2), lax.rem(lax.div(s, 2), 4), lax.div(s, 8)
    xl, z = lax.div(g, 4), lax.rem(g, 4)
    x = xh * 2 + xl
    nc = 1 - c
    unit = c * y + nc * z
    unit2 = nc * y + c * z
    local = nc * xl + c * xh

    def dev(xh_, y_, c_, xl_, z_):
        return ((xh_ * 4 + y_) * 2 + c_, xl_ * 4 + z_)

    def along(dy, dz):
        return dev(xh, lax.rem(y + dy, 4), c, xl, lax.rem(z + dz, 4))

    def across(dx):
        nx = lax.rem(x + dx, 4)
        return dev(lax.div(nx, 2), y, c, lax.rem(nx, 2), z)

    right, left = along(c, nc), along(3 * c, 3 * nc)
    right2, left2 = along(nc, c), along(3 * nc, 3 * c)
    right_x, left_x = across(1), across(3)

    barrier = pltpu.get_barrier_semaphore()
    peers = [right, left, right2, left2, right_x, left_x, dev(xh, y, nc, xl, z)]
    for b in range(2):
        peers.append(dev(xh, y, b, 1 - xl, z))
        peers.append(dev(1 - xh, y, b, xl, z))
        for a in range(2):
            peers.append(dev(xh, z, a, b, y))
    for to in peers:
        pl.semaphore_signal(barrier, inc=1, device_id=to, device_id_type=MESH)

    def remote(src, dst, i, j, to):
        return pltpu.make_async_remote_copy(
            src_ref=src, dst_ref=dst, send_sem=snd.at[i], recv_sem=rcv.at[j],
            device_id=to, device_id_type=MESH,
        )

    sends = []

    def put(src, dst, i, j, to):
        mine = jnp.logical_and(to[0] == s, to[1] == g)
        copy = remote(src, dst, i, j, to)

        @pl.when(mine)
        def _():
            pltpu.make_async_copy(src, dst, rcv.at[j]).start()

        @pl.when(jnp.logical_not(mine))
        def _():
            copy.start()

        sends.append((copy, jnp.logical_not(mine)))

    def arrived(dst, j):
        pltpu.make_async_copy(dst, dst, rcv.at[j]).wait()

    def start(copy):
        copy.start()
        sends.append((copy, None))

    class Ring:
        def __init__(self, view, at, to_right, to_left, base):
            self.view, self.base = view, base
            self.to = (to_right, to_left)
            self.units = (at, lax.rem(at + 3, 4), lax.rem(at + 1, 4), lax.rem(at + 2, 4))

        def send(self, u, half, k, side):
            ref = self.view(self.units[u], half)
            start(remote(ref, ref, self.base + k, self.base + k, self.to[side]))

        def wait(self, *slots):
            for k in slots:
                u, half = ((1, 0), (1, 1), (3, 0), (2, 1), (2, 0), (3, 1))[k]
                arrived(self.view(self.units[u], half), self.base + k)

        def begin(self):
            self.send(0, 0, 0, 0)
            self.send(0, 1, 3, 1)
            self.send(0, 1, 1, 0)
            self.send(0, 0, 4, 1)

        def forward(self):
            self.wait(0)
            self.send(1, 0, 2, 0)
            self.wait(3)
            self.send(2, 1, 5, 1)

        def forward_x(self):
            unit_ = (1 - xl) * self.units[2] + xl * self.units[1]
            to = tuple((1 - xl) * b + xl * a for a, b in zip(*self.to))
            for half, slot in ((0, 4 * (1 - xl)), (1, 3 - 2 * xl)):
                ref, k = self.view(unit_, half), self.base + 2 + 3 * half
                arrived(ref, self.base + slot)
                start(remote(ref, ref, k, k, to))

        def near_x(self):
            unit_ = (1 - xl) * self.units[1] + xl * self.units[2]
            for half, slot in ((0, 4 * xl), (1, 1 + 2 * xl)):
                arrived(self.view(unit_, half), self.base + slot)

    def token_ring(part_, base):
        return Ring(
            lambda u, h: xs.at[u, pl.ds((part_ * 2 + h) * 128, 128)], unit, right, left, base
        )

    def weight_rings(w, base):
        return (
            Ring(
                lambda u, h: w.at[xl, xh, 0, :, pl.ds(u * 128 + h * 64, 64)],
                unit2, right2, left2, base,
            ),
            Ring(
                lambda u, h: w.at[lax.rem(u, 2), lax.div(u, 2), 0, :, pl.ds(h * 256, 256)],
                x, right_x, left_x, base + 6,
            ),
            Ring(
                lambda u, h: w.at[
                    lax.rem(u, 2), lax.div(u, 2), 1, :, pl.ds(unit2 * 128 + h * 64, 64)
                ],
                x, right_x, left_x, base + 12,
            ),
            Ring(
                lambda u, h: w.at[1 - xl, h, 1, :, pl.ds(u * 128, 128)],
                unit2, right2, left2, base + 18,
            ),
            Ring(
                lambda u, h: w.at[xl, h, 1, :, pl.ds(u * 128, 128)],
                unit2, right2, left2, base + 24,
            ),
        )

    tok_l, tok_r = token_ring(local, RING_TL), token_ring(1 - local, RING_TR)
    w1a, w1b, w2a, w2b, w2c = weight_rings(wg, RING_W)
    o1a, o1b, o2a, o2b, o2c = weight_rings(wo, RING_O)

    def norm_half(h):
        def norm_rows(k, _):
            rows = pl.ds(pl.multiple_of(h * 128 + k * 32, 32), 32)
            v = tok[rows, :].astype(F32)
            scale = lax.rsqrt(jnp.mean(v * v, axis=-1, keepdims=True) + EPS)
            v = (v * scale * norm_gain[...]).astype(BF16)
            for old in range(16):
                new = (old // 8 * 2 + old % 2) * 4 + old // 2 % 4
                nrm[rows, new * 128 : new * 128 + 128] = v[:, old * 128 : old * 128 + 128]
            return 0

        lax.fori_loop(0, 4, norm_rows, 0)

    norm_half(0)
    norm_half(1)
    pl.semaphore_wait(barrier, len(peers))

    to_s, to_t = dev(xh, y, 0, xl, z), dev(xh, z, 1, xl, y)
    mine_w, mine_o = (w.at[xl, xh, c, :, pl.ds(y * 128, 128)] for w in (wg, wo))
    put(w_s, mine_w, WGT, WGT + c, to_s)
    put(w_t, mine_w, WGT + 1, WGT + c, to_t)
    for h in range(2):
        src = nrm.at[pl.ds(h * 128, 128)]
        i_s, i_t = xl * 2 + h, xh * 2 + c
        put(src, xs.at[z, pl.ds(i_s * 128, 128)], TOK + h, TOK + i_s, dev(xh, y, 0, c, z))
        put(src, xs.at[y, pl.ds(i_t * 128, 128)], TOK + 2 + h, TOK + i_t, dev(h, y, 1, xl, z))
    for b in range(2):
        wo_own[b, 0] = w_o[...].astype(F32)[:, b, :].astype(BF16)
    put(wo_own.at[0], mine_o, OUTW, OUTW + c, to_s)
    put(wo_own.at[1], mine_o, OUTW + 1, OUTW + c, to_t)
    for h in range(2):
        put(
            gain.at[c], gn.at[xl], GAIN + h, GAIN + xl,
            dev(xh, nc * y + c * z, c, h, nc * z + c * y),
        )

    def rows_arrived(w, i, slot):
        arrived(w.at[xl, xh, i, :, pl.ds(unit2 * 128, 128)], slot + i)

    def tokens_arrived(half):
        for h in range(2):
            i = half * 2 + h
            arrived(xs.at[unit, pl.ds(i * 128, 128)], TOK + i)

    tokens_arrived(local)
    tok_l.begin()
    rows_arrived(wg, 0, WGT)
    w1a.begin()
    rows_arrived(wg, 1, WGT)
    w2a.begin()
    tok_l.forward()
    w1a.forward()
    tokens_arrived(1 - local)
    tok_r.begin()
    w2a.forward()
    for i in range(2):
        rows_arrived(wo, i, OUTW)
    o1a.begin()
    o2a.begin()
    w1a.wait(1, 4, 2, 5)
    w1b.begin()
    w2a.wait(1, 4, 2, 5)
    w2b.begin()
    tok_r.forward()
    o1a.forward()
    o2a.forward()
    w2b.forward()
    w1b.forward_x()
    w2c.begin()
    tok_l.wait(1, 4, 2, 5)
    for i in range(2):
        arrived(gn.at[i], GAIN + i)
    tok_r.wait(1, 4, 2, 5)
    w1b.near_x()
    w2b.wait(1, 4, 2, 5)

    def project(pair, first, last):
        def one(role, u, _):
            w = [wg[pair, :, :, n].reshape(2048, 256) for n in range(3)]
            acc = mm(xs[u], jnp.concatenate(w, axis=1))
            for n in range(3):
                for j in range(2):
                    a = acc[:, n * 256 + j * 128 : n * 256 + j * 128 + 128]
                    if n < 2:
                        a = a * lax.rsqrt(jnp.mean(a * a, axis=-1, keepdims=True) + EPS)
                        a = a * gn[pair, 2 * n + j : 2 * n + j + 1, :]
                    if n == 0:
                        a = a * (128 ** -0.5)

                    if role == 0:
                        b = a.astype(BF16)
                        for k in range(8):
                            i, f = k // 2, k % 2
                            at = f * 64 + ((i // 2) * 4 + u) * 8 + i % 2 * 4
                            qkv[n, pair * 2 + j, pl.ds(at, 4)] = b[
                                k * 64 : k * 64 + 64
                            ].reshape(4, 16, 128)
                    else:
                        for i in range(4):
                            for m in range(8):
                                at = i * 128 + m * 8
                                b = jnp.concatenate([a[at : at + 8], a[at + 64 : at + 72]], axis=0)
                                at = m * 16 + ((i // 2) * 4 + u) * 2 + i % 2
                                qkv[n, pair * 2 + j, at] = b.astype(BF16)
            return 0

        for role in range(2):
            @pl.when(c == role)
            def _():
                lax.fori_loop(first, last, lambda u, v: one(role, u, v), 0)

    def softmax_mix(sc, v):
        e = jnp.exp(sc - jnp.max(sc, axis=-1, keepdims=True)).astype(BF16)
        o = mm(e, jnp.concatenate([v, jnp.ones_like(v)], axis=1))
        return o[:, 0:128] / o[:, 128:256]

    def tile(n, hd, first, rows=128):
        return qkv[n, hd, pl.ds(first, rows // 16)].reshape(rows, 128)

    def attend(pair, half):
        @pl.when(c == 0)
        def _():
            def spatial(k, _):
                t = half * 4 + k
                for f in range(2):
                    at = [f * 64 + win[j, t] * 8 for j in range(4)]
                    for j in range(2):
                        hd = pair * 2 + j
                        q = tile(0, hd, f * 64 + t * 8)
                        keys = jnp.concatenate([tile(1, hd, a) for a in at], axis=0)
                        vals = jnp.concatenate([tile(2, hd, a) for a in at], axis=0)
                        o = softmax_mix(mm_t(q, keys), vals).astype(BF16)
                        for h in range(2):
                            att[
                                pair, k, half * 4 + h * 2 + f, :, j * 128 : j * 128 + 128
                            ] = o[h * 64 : h * 64 + 64]
                return 0

            lax.fori_loop(0, 4, spatial, 0)

        for b in range(2):
            @pl.when(jnp.logical_and(c == 1, half == b))
            def _():
                def temporal(pg, _):
                    rows = pl.ds(pl.multiple_of(pg * 16, 16), 16)
                    keys = 128 * (b + 1)
                    qi = lax.broadcasted_iota(jnp.int32, (128, keys), 0) + b * 128
                    ki = lax.broadcasted_iota(jnp.int32, (128, keys), 1)
                    ok = jnp.logical_and(
                        jnp.bitwise_and(qi, 7) == jnp.bitwise_and(ki, 7), ki <= qi
                    )
                    for j in range(2):
                        hd = pair * 2 + j
                        res = []
                        for m in range(2):
                            first = pg * 32 + m * 16
                            q = tile(0, hd, first + b * 8)
                            sc = mm_t(q, tile(1, hd, first, keys))
                            res.append(
                                softmax_mix(jnp.where(ok, sc, -1e30), tile(2, hd, first, keys))
                            )
                        for m in range(16):
                            fr = b * 16 + m
                            i = b * 2 + (fr // 2) % 2
                            o = jnp.concatenate([v[m * 8 : m * 8 + 8] for v in res], axis=0)
                            att[
                                pair, fr // 4 % 4, i * 2 + fr % 2, rows, j * 128 : j * 128 + 128
                            ] = o.astype(BF16)
                    return 0

                lax.fori_loop(0, 4, temporal, 0)

    project(1 - xl, 0, 2)
    w2c.forward()
    o1a.wait(1, 4, 2, 5)
    o1b.begin()
    o2a.wait(1, 4, 2, 5)
    o2b.begin()
    o2c.begin()
    project(1 - xl, 2, 4)
    attend(1 - xl, 0)
    o1b.forward_x()
    o2b.forward()
    o2c.forward()
    attend(1 - xl, 1)
    w1b.wait(2, 5)
    w2c.wait(1, 4, 2, 5)
    project(xl, 0, 2)
    project(xl, 2, 4)
    attend(xl, 1 - local)
    o1b.near_x()
    o1b.wait(2, 5)
    o2b.wait(1, 4, 2, 5)
    o2c.wait(1, 4, 2, 5)

    def outproj(u, half):
        def one(k, _):
            rows = pl.ds(pl.multiple_of(half * 256, 256), 256)
            o = [att[p, u, pl.ds(half * 4, 4)].reshape(256, 256) for p in range(2)]
            for b in range(2):
                acc = mm_t(o[0], wo[0, k, b, 0]) + mm_t(o[1], wo[1, k, b, 0])
                for q in range(4):
                    cols = pl.ds(pl.multiple_of(k * 1024 + q * 256 + b * 128, 128), 128)
                    part[u, rows, cols] = acc[:, q * 128 : q * 128 + 128].astype(BF16)
            return 0

        lax.fori_loop(0, 2, one, 0)

    def add_rows(u, first, *others):
        def one(k, _):
            rows = pl.ds(pl.multiple_of(first + k * 32, 32), 32)
            here = pl.ds(pl.multiple_of(k * 32, 32), 32)
            total = part[u, rows, :].astype(F32)
            for other in others:
                total = total + other[here, :].astype(F32)
            part[u, rows, :] = total.astype(BF16)
            return 0

        lax.fori_loop(0, 2, one, 0)

    u_l, u_r, u_2 = lax.rem(unit + 3, 4), lax.rem(unit + 1, 4), lax.rem(unit + 2, 4)
    pieces = [(1 - local) * 2, (1 - local) * 2 + 1, local * 2, local * 2 + 1]

    def reduce_send(n, u, q, dst, k, to):
        src = part.at[u, pl.ds(pieces[n] * 128 + q * 64, 64)]
        start(remote(src, dst, RS + n * 6 + k, RS + n * 6 + k, to))

    def reduce_start(half, n):
        outproj(u_2, half)
        reduce_send(n, u_2, 0, rs1.at[n, 0], 0, right)
        reduce_send(n, u_2, 1, rs1.at[n, 1], 1, left)
        outproj(u_r, half)
        reduce_send(n, u_r, 1, rs2.at[n, 0, 1], 2, right)
        outproj(u_l, half)
        reduce_send(n, u_l, 0, rs2.at[n, 1, 0], 3, left)
        reduce_send(n + 1, u_2, 0, rs1.at[n + 1, 0], 0, right)
        reduce_send(n + 1, u_2, 1, rs1.at[n + 1, 1], 1, left)
        reduce_send(n + 1, u_r, 1, rs2.at[n + 1, 0, 1], 2, right)
        reduce_send(n + 1, u_l, 0, rs2.at[n + 1, 1, 0], 3, left)

    def reduce_pass(n):
        arrived(rs1.at[n, 0], RS + n * 6)
        add_rows(u_r, pieces[n] * 128, rs1.at[n, 0])
        reduce_send(n, u_r, 0, rs2.at[n, 0, 0], 4, right)
        arrived(rs1.at[n, 1], RS + n * 6 + 1)
        add_rows(u_l, pieces[n] * 128 + 64, rs1.at[n, 1])
        reduce_send(n, u_l, 1, rs2.at[n, 1, 1], 5, left)

    def reduce_end(half, n):
        h = n % 2
        for q in range(2):
            arrived(rs2.at[n, 1 - q, q], RS + n * 6 + 3 - q)
            arrived(rs2.at[n, q, q], RS + n * 6 + 4 + q)
            add_rows(unit, pieces[n] * 128 + q * 64, rs2.at[n, 0, q], rs2.at[n, 1, q])
        at = nc * h + c * (2 + xh)
        to = dev(nc * xh + c * half, y, nc * xl + c * h, nc * half + c * xl, z)
        put(part.at[unit, pl.ds(pieces[n] * 128, 128)], fin.at[at], FIN + n, FIN + at, to)

    reduce_start(1 - local, 0)
    attend(xl, local)
    reduce_pass(0)
    reduce_pass(1)
    outproj(unit, 1 - local)
    reduce_start(local, 2)
    reduce_end(1 - local, 0)
    reduce_end(1 - local, 1)
    reduce_pass(2)
    reduce_pass(3)
    outproj(unit, local)
    reduce_end(local, 2)
    reduce_end(local, 3)

    for h in range(2):
        arrived(fin.at[h], FIN + h)
        arrived(fin.at[2 + h], FIN + 2 + h)

        def total_rows(k, _):
            rows = pl.ds(pl.multiple_of(k * 32, 32), 32)
            here = pl.ds(pl.multiple_of(h * 128 + k * 32, 32), 32)
            total = fin[h, rows, :].astype(F32) + fin[2 + h, rows, :].astype(F32)
            out[here, :] = (tok[here, :].astype(F32) + total).astype(BF16)
            return 0

        lax.fori_loop(0, 4, total_rows, 0)

    for copy, cond in sends:
        if cond is None:
            copy.wait_send()
        else:
            pl.when(cond)(copy.wait_send)


def body(tokens, norm_gain, qk_gain, window_blocks, w_spatial, w_temporal, w_out):
    rows, frames, width = tokens.shape
    tok = tokens.reshape(2, 64, 2, width).transpose(0, 2, 1, 3).reshape(256, width)
    vmem = pl.BlockSpec(memory_space=pltpu.VMEM)
    res = pl.pallas_call(
        kernel,
        name="attention_block",
        out_shape=pltpu.VMEM((256, width), BF16),
        in_specs=[pl.BlockSpec(memory_space=pltpu.SMEM)] + [vmem] * 6,
        out_specs=vmem,
        scratch_shapes=[
            pltpu.VMEM((256, 2048), BF16),
            pltpu.VMEM((2, 1, 128, 256), BF16),
            pltpu.VMEM((4, 512, 2048), BF16),
            pltpu.VMEM((2, 2, 2, 3, 512, 256), BF16),
            pltpu.VMEM((2, 2, 2, 1, 512, 256), BF16),
            pltpu.VMEM((2, 4, 128), F32),
            pltpu.VMEM((3, 4, 128, 16, 128), BF16),
            pltpu.VMEM((2, 4, 8, 64, 256), BF16),
            pltpu.VMEM((4, 512, 2048), BF16),
            pltpu.VMEM((4, 2, 64, 2048), BF16),
            pltpu.VMEM((4, 2, 2, 64, 2048), BF16),
            pltpu.VMEM((4, 128, 2048), BF16),
            pltpu.SemaphoreType.DMA((SLOTS,)),
            pltpu.SemaphoreType.DMA((SLOTS,)),
        ],
        compiler_params=pltpu.CompilerParams(
            collective_id=0, has_side_effects=True, vmem_limit_bytes=60 * 1024 * 1024
        ),
    )(
        window_blocks.T,
        pltpu.with_memory_space_constraint(tok, pltpu.VMEM),
        norm_gain.reshape(1, width),
        qk_gain.reshape(2, 4, 128),
        w_spatial.transpose(1, 0, 2),
        w_temporal.transpose(1, 0, 2),
        w_out,
    )
    return res.reshape(2, 2, 64, width).transpose(0, 2, 1, 3).reshape(rows, frames, width)


def solution(mesh):
    return jax.shard_map(
        body,
        mesh=mesh,
        in_specs=(
            P("grp", "seq", None),
            P(),
            P(None, None, "grp", None),
            P(),
            P("seq", None, "grp"),
            P("seq", None, "grp"),
            P("seq", None, "grp"),
        ),
        out_specs=P("grp", "seq", None),
        check_vma=False,
    )
```

```python
import jax
import jax.numpy as jnp
from jax import lax
from jax.experimental import pallas as pl
from jax.experimental.pallas import tpu as pltpu
from jax.sharding import PartitionSpec as P

MESH = pl.DeviceIdType.MESH
EPS = 1e-06
F32 = jnp.float32
BF16 = jnp.bfloat16

TOK, WGT, OUTW, GAIN, RING_TL, RING_TR, RING_W, RING_O, RS, FIN = (
    0, 4, 6, 8, 10, 16, 22, 52, 82, 106,
)
SLOTS = 110


def mm(a, b):
    return jnp.dot(a, b, preferred_element_type=F32)


def mm_t(a, b):
    return lax.dot_general(a, b, (((1,), (1,)), ((), ())), preferred_element_type=F32)


def kernel(
    win, tok, norm_gain, gain, w_s, w_t, w_o, out,
    nrm, wo_own, xs, wg, wo, gn, qkv, att, part, rs1, rs2, fin, snd, rcv,
):
    s, g = lax.axis_index("seq"), lax.axis_index("grp")
    c, y, xh = lax.rem(s, 2), lax.rem(lax.div(s, 2), 4), lax.div(s, 8)
    xl, z = lax.div(g, 4), lax.rem(g, 4)
    x = xh * 2 + xl
    nc = 1 - c
    unit = c * y + nc * z
    unit2 = nc * y + c * z
    local = nc * xl + c * xh

    def dev(xh_, y_, c_, xl_, z_):
        return ((xh_ * 4 + y_) * 2 + c_, xl_ * 4 + z_)

    def along(dy, dz):
        return dev(xh, lax.rem(y + dy, 4), c, xl, lax.rem(z + dz, 4))

    def across(dx):
        nx = lax.rem(x + dx, 4)
        return dev(lax.div(nx, 2), y, c, lax.rem(nx, 2), z)

    right, left = along(c, nc), along(3 * c, 3 * nc)
    right2, left2 = along(nc, c), along(3 * nc, 3 * c)
    right_x, left_x = across(1), across(3)

    barrier = pltpu.get_barrier_semaphore()
    peers = [right, left, right2, left2, right_x, left_x, dev(xh, y, nc, xl, z)]
    for b in range(2):
        peers.append(dev(xh, y, b, 1 - xl, z))
        peers.append(dev(1 - xh, y, b, xl, z))
        for a in range(2):
            peers.append(dev(xh, z, a, b, y))
    for to in peers:
        pl.semaphore_signal(barrier, inc=1, device_id=to, device_id_type=MESH)

    def remote(src, dst, i, j, to):
        return pltpu.make_async_remote_copy(
            src_ref=src, dst_ref=dst, send_sem=snd.at[i], recv_sem=rcv.at[j],
            device_id=to, device_id_type=MESH,
        )

    sends = []

    def put(src, dst, i, j, to):
        mine = jnp.logical_and(to[0] == s, to[1] == g)
        copy = remote(src, dst, i, j, to)

        @pl.when(mine)
        def _():
            pltpu.make_async_copy(src, dst, rcv.at[j]).start()

        @pl.when(jnp.logical_not(mine))
        def _():
            copy.start()

        sends.append((copy, jnp.logical_not(mine)))

    def arrived(dst, j):
        pltpu.make_async_copy(dst, dst, rcv.at[j]).wait()

    def start(copy):
        copy.start()
        sends.append((copy, None))

    class Ring:
        def __init__(self, view, at, to_right, to_left, base):
            self.view, self.base = view, base
            self.to = (to_right, to_left)
            self.units = (at, lax.rem(at + 3, 4), lax.rem(at + 1, 4), lax.rem(at + 2, 4))

        def send(self, u, half, k, side):
            ref = self.view(self.units[u], half)
            start(remote(ref, ref, self.base + k, self.base + k, self.to[side]))

        def wait(self, *slots):
            for k in slots:
                u, half = ((1, 0), (1, 1), (3, 0), (2, 1), (2, 0), (3, 1))[k]
                arrived(self.view(self.units[u], half), self.base + k)

        def begin(self):
            self.send(0, 0, 0, 0)
            self.send(0, 1, 3, 1)
            self.send(0, 1, 1, 0)
            self.send(0, 0, 4, 1)

        def forward(self):
            self.wait(0)
            self.send(1, 0, 2, 0)
            self.wait(3)
            self.send(2, 1, 5, 1)

        def forward_x(self):
            unit_ = (1 - xl) * self.units[2] + xl * self.units[1]
            to = tuple((1 - xl) * b + xl * a for a, b in zip(*self.to))
            for half, slot in ((0, 4 * (1 - xl)), (1, 3 - 2 * xl)):
                ref, k = self.view(unit_, half), self.base + 2 + 3 * half
                arrived(ref, self.base + slot)
                start(remote(ref, ref, k, k, to))

        def near_x(self):
            unit_ = (1 - xl) * self.units[1] + xl * self.units[2]
            for half, slot in ((0, 4 * xl), (1, 1 + 2 * xl)):
                arrived(self.view(unit_, half), self.base + slot)

    def token_ring(part_, base):
        return Ring(
            lambda u, h: xs.at[u, pl.ds((part_ * 2 + h) * 128, 128)], unit, right, left, base
        )

    def weight_rings(w, base):
        return (
            Ring(
                lambda u, h: w.at[xl, xh, 0, :, pl.ds(u * 128 + h * 64, 64)],
                unit2, right2, left2, base,
            ),
            Ring(
                lambda u, h: w.at[lax.rem(u, 2), lax.div(u, 2), 0, :, pl.ds(h * 256, 256)],
                x, right_x, left_x, base + 6,
            ),
            Ring(
                lambda u, h: w.at[
                    lax.rem(u, 2), lax.div(u, 2), 1, :, pl.ds(unit2 * 128 + h * 64, 64)
                ],
                x, right_x, left_x, base + 12,
            ),
            Ring(
                lambda u, h: w.at[1 - xl, h, 1, :, pl.ds(u * 128, 128)],
                unit2, right2, left2, base + 18,
            ),
            Ring(
                lambda u, h: w.at[xl, h, 1, :, pl.ds(u * 128, 128)],
                unit2, right2, left2, base + 24,
            ),
        )

    tok_l, tok_r = token_ring(local, RING_TL), token_ring(1 - local, RING_TR)
    w1a, w1b, w2a, w2b, w2c = weight_rings(wg, RING_W)
    o1a, o1b, o2a, o2b, o2c = weight_rings(wo, RING_O)

    def norm_half(h):
        def norm_rows(k, _):
            rows = pl.ds(pl.multiple_of(h * 128 + k * 32, 32), 32)
            v = tok[rows, :].astype(F32)
            scale = lax.rsqrt(jnp.mean(v * v, axis=-1, keepdims=True) + EPS)
            v = (v * scale * norm_gain[...]).astype(BF16)
            for old in range(16):
                new = (old // 8 * 2 + old % 2) * 4 + old // 2 % 4
                nrm[rows, new * 128 : new * 128 + 128] = v[:, old * 128 : old * 128 + 128]
            return 0

        lax.fori_loop(0, 4, norm_rows, 0)

    norm_half(0)
    norm_half(1)
    pl.semaphore_wait(barrier, len(peers))

    to_s, to_t = dev(xh, y, 0, xl, z), dev(xh, z, 1, xl, y)
    mine_w, mine_o = (w.at[xl, xh, c, :, pl.ds(y * 128, 128)] for w in (wg, wo))
    put(w_s, mine_w, WGT, WGT + c, to_s)
    put(w_t, mine_w, WGT + 1, WGT + c, to_t)
    for h in range(2):
        src = nrm.at[pl.ds(h * 128, 128)]
        i_s, i_t = xl * 2 + h, xh * 2 + c
        put(src, xs.at[z, pl.ds(i_s * 128, 128)], TOK + h, TOK + i_s, dev(xh, y, 0, c, z))
        put(src, xs.at[y, pl.ds(i_t * 128, 128)], TOK + 2 + h, TOK + i_t, dev(h, y, 1, xl, z))
    for b in range(2):
        wo_own[b, 0] = w_o[...].astype(F32)[:, b, :].astype(BF16)
    put(wo_own.at[0], mine_o, OUTW, OUTW + c, to_s)
    put(wo_own.at[1], mine_o, OUTW + 1, OUTW + c, to_t)
    for h in range(2):
        put(
            gain.at[c], gn.at[xl], GAIN + h, GAIN + xl,
            dev(xh, nc * y + c * z, c, h, nc * z + c * y),
        )

    def rows_arrived(w, i, slot):
        arrived(w.at[xl, xh, i, :, pl.ds(unit2 * 128, 128)], slot + i)

    def tokens_arrived(half):
        for h in range(2):
            i = half * 2 + h
            arrived(xs.at[unit, pl.ds(i * 128, 128)], TOK + i)

    tokens_arrived(local)
    tok_l.begin()
    rows_arrived(wg, 0, WGT)
    w1a.begin()
    rows_arrived(wg, 1, WGT)
    w2a.begin()
    tok_l.forward()
    w1a.forward()
    tokens_arrived(1 - local)
    tok_r.begin()
    w2a.forward()
    for i in range(2):
        rows_arrived(wo, i, OUTW)
    o1a.begin()
    o2a.begin()
    w1a.wait(1, 4, 2, 5)
    w1b.begin()
    w2a.wait(1, 4, 2, 5)
    w2b.begin()
    tok_r.forward()
    o1a.forward()
    o2a.forward()
    w2b.forward()
    w1b.forward_x()
    w2c.begin()
    tok_l.wait(1, 4, 2, 5)
    for i in range(2):
        arrived(gn.at[i], GAIN + i)
    tok_r.wait(1, 4, 2, 5)
    w1b.near_x()
    w2b.wait(1, 4, 2, 5)

    def project(pair, first, last):
        def one(role, u, _):
            w = [wg[pair, :, :, n].reshape(2048, 256) for n in range(3)]
            acc = mm(xs[u], jnp.concatenate(w, axis=1))
            for n in range(3):
                for j in range(2):
                    a = acc[:, n * 256 + j * 128 : n * 256 + j * 128 + 128]
                    if n < 2:
                        a = a * lax.rsqrt(jnp.mean(a * a, axis=-1, keepdims=True) + EPS)
                        a = a * gn[pair, 2 * n + j : 2 * n + j + 1, :]
                    if n == 0:
                        a = a * (128 ** -0.5)

                    if role == 0:
                        b = a.astype(BF16)
                        for k in range(8):
                            i, f = k // 2, k % 2
                            at = f * 64 + ((i // 2) * 4 + u) * 8 + i % 2 * 4
                            qkv[n, pair * 2 + j, pl.ds(at, 4)] = b[
                                k * 64 : k * 64 + 64
                            ].reshape(4, 16, 128)
                    else:
                        for i in range(4):
                            for m in range(8):
                                at = i * 128 + m * 8
                                b = jnp.concatenate([a[at : at + 8], a[at + 64 : at + 72]], axis=0)
                                at = m * 16 + ((i // 2) * 4 + u) * 2 + i % 2
                                qkv[n, pair * 2 + j, at] = b.astype(BF16)
            return 0

        for role in range(2):
            @pl.when(c == role)
            def _():
                lax.fori_loop(first, last, lambda u, v: one(role, u, v), 0)

    def softmax_mix(sc, v):
        e = jnp.exp(sc - jnp.max(sc, axis=-1, keepdims=True)).astype(BF16)
        o = mm(e, jnp.concatenate([v, jnp.ones_like(v)], axis=1))
        return o[:, 0:128] / o[:, 128:256]

    def tile(n, hd, first, rows=128):
        return qkv[n, hd, pl.ds(first, rows // 16)].reshape(rows, 128)

    def attend(pair, half):
        @pl.when(c == 0)
        def _():
            def spatial(k, _):
                t = half * 4 + k
                for f in range(2):
                    at = [f * 64 + win[j, t] * 8 for j in range(4)]
                    for j in range(2):
                        hd = pair * 2 + j
                        q = tile(0, hd, f * 64 + t * 8)
                        keys = jnp.concatenate([tile(1, hd, a) for a in at], axis=0)
                        vals = jnp.concatenate([tile(2, hd, a) for a in at], axis=0)
                        o = softmax_mix(mm_t(q, keys), vals).astype(BF16)
                        for h in range(2):
                            att[
                                pair, k, half * 4 + h * 2 + f, :, j * 128 : j * 128 + 128
                            ] = o[h * 64 : h * 64 + 64]
                return 0

            lax.fori_loop(0, 4, spatial, 0, unroll=2)

        for b in range(2):
            @pl.when(jnp.logical_and(c == 1, half == b))
            def _():
                def temporal(pg, _):
                    rows = pl.ds(pl.multiple_of(pg * 16, 16), 16)
                    keys = 128 * (b + 1)
                    qi = lax.broadcasted_iota(jnp.int32, (128, keys), 0) + b * 128
                    ki = lax.broadcasted_iota(jnp.int32, (128, keys), 1)
                    ok = jnp.logical_and(
                        jnp.bitwise_and(qi, 7) == jnp.bitwise_and(ki, 7), ki <= qi
                    )
                    for j in range(2):
                        hd = pair * 2 + j
                        res = []
                        for m in range(2):
                            first = pg * 32 + m * 16
                            q = tile(0, hd, first + b * 8)
                            sc = mm_t(q, tile(1, hd, first, keys))
                            res.append(
                                softmax_mix(jnp.where(ok, sc, -1e30), tile(2, hd, first, keys))
                            )
                        for m in range(16):
                            fr = b * 16 + m
                            i = b * 2 + (fr // 2) % 2
                            o = jnp.concatenate([v[m * 8 : m * 8 + 8] for v in res], axis=0)
                            att[
                                pair, fr // 4 % 4, i * 2 + fr % 2, rows, j * 128 : j * 128 + 128
                            ] = o.astype(BF16)
                    return 0

                lax.fori_loop(0, 4, temporal, 0, unroll=2)

    project(1 - xl, 0, 2)
    w2c.forward()
    o1a.wait(1, 4, 2, 5)
    o1b.begin()
    o2a.wait(1, 4, 2, 5)
    o2b.begin()
    o2c.begin()
    project(1 - xl, 2, 4)
    attend(1 - xl, 0)
    o1b.forward_x()
    o2b.forward()
    o2c.forward()
    attend(1 - xl, 1)
    w1b.wait(2, 5)
    w2c.wait(1, 4, 2, 5)
    project(xl, 0, 2)
    project(xl, 2, 4)
    attend(xl, 1 - local)
    o1b.near_x()
    o1b.wait(2, 5)
    o2b.wait(1, 4, 2, 5)
    o2c.wait(1, 4, 2, 5)

    def outproj(u, half):
        def one(k, _):
            rows = pl.ds(pl.multiple_of(half * 256, 256), 256)
            o = [att[p, u, pl.ds(half * 4, 4)].reshape(256, 256) for p in range(2)]
            for b in range(2):
                acc = mm_t(o[0], wo[0, k, b, 0]) + mm_t(o[1], wo[1, k, b, 0])
                for q in range(4):
                    cols = pl.ds(pl.multiple_of(k * 1024 + q * 256 + b * 128, 128), 128)
                    part[u, rows, cols] = acc[:, q * 128 : q * 128 + 128].astype(BF16)
            return 0

        lax.fori_loop(0, 2, one, 0)

    def add_rows(u, first, *others):
        def one(k, _):
            rows = pl.ds(pl.multiple_of(first + k * 32, 32), 32)
            here = pl.ds(pl.multiple_of(k * 32, 32), 32)
            total = part[u, rows, :].astype(F32)
            for other in others:
                total = total + other[here, :].astype(F32)
            part[u, rows, :] = total.astype(BF16)
            return 0

        lax.fori_loop(0, 2, one, 0)

    u_l, u_r, u_2 = lax.rem(unit + 3, 4), lax.rem(unit + 1, 4), lax.rem(unit + 2, 4)
    pieces = [(1 - local) * 2, (1 - local) * 2 + 1, local * 2, local * 2 + 1]

    def reduce_send(n, u, q, dst, k, to):
        src = part.at[u, pl.ds(pieces[n] * 128 + q * 64, 64)]
        start(remote(src, dst, RS + n * 6 + k, RS + n * 6 + k, to))

    def reduce_start(half, n):
        outproj(u_2, half)
        reduce_send(n, u_2, 0, rs1.at[n, 0], 0, right)
        reduce_send(n, u_2, 1, rs1.at[n, 1], 1, left)
        outproj(u_r, half)
        reduce_send(n, u_r, 1, rs2.at[n, 0, 1], 2, right)
        outproj(u_l, half)
        reduce_send(n, u_l, 0, rs2.at[n, 1, 0], 3, left)
        reduce_send(n + 1, u_2, 0, rs1.at[n + 1, 0], 0, right)
        reduce_send(n + 1, u_2, 1, rs1.at[n + 1, 1], 1, left)
        reduce_send(n + 1, u_r, 1, rs2.at[n + 1, 0, 1], 2, right)
        reduce_send(n + 1, u_l, 0, rs2.at[n + 1, 1, 0], 3, left)

    def reduce_pass(n):
        arrived(rs1.at[n, 0], RS + n * 6)
        add_rows(u_r, pieces[n] * 128, rs1.at[n, 0])
        reduce_send(n, u_r, 0, rs2.at[n, 0, 0], 4, right)
        arrived(rs1.at[n, 1], RS + n * 6 + 1)
        add_rows(u_l, pieces[n] * 128 + 64, rs1.at[n, 1])
        reduce_send(n, u_l, 1, rs2.at[n, 1, 1], 5, left)

    def reduce_end(half, n):
        h = n % 2
        for q in range(2):
            arrived(rs2.at[n, 1 - q, q], RS + n * 6 + 3 - q)
            arrived(rs2.at[n, q, q], RS + n * 6 + 4 + q)
            add_rows(unit, pieces[n] * 128 + q * 64, rs2.at[n, 0, q], rs2.at[n, 1, q])
        at = nc * h + c * (2 + xh)
        to = dev(nc * xh + c * half, y, nc * xl + c * h, nc * half + c * xl, z)
        put(part.at[unit, pl.ds(pieces[n] * 128, 128)], fin.at[at], FIN + n, FIN + at, to)

    reduce_start(1 - local, 0)
    attend(xl, local)
    reduce_pass(0)
    reduce_pass(1)
    outproj(unit, 1 - local)
    reduce_start(local, 2)
    reduce_end(1 - local, 0)
    reduce_end(1 - local, 1)
    reduce_pass(2)
    reduce_pass(3)
    outproj(unit, local)
    reduce_end(local, 2)
    reduce_end(local, 3)

    for h in range(2):
        arrived(fin.at[h], FIN + h)
        arrived(fin.at[2 + h], FIN + 2 + h)

        def total_rows(k, _):
            rows = pl.ds(pl.multiple_of(k * 32, 32), 32)
            here = pl.ds(pl.multiple_of(h * 128 + k * 32, 32), 32)
            total = fin[h, rows, :].astype(F32) + fin[2 + h, rows, :].astype(F32)
            out[here, :] = (tok[here, :].astype(F32) + total).astype(BF16)
            return 0

        lax.fori_loop(0, 4, total_rows, 0)

    for copy, cond in sends:
        if cond is None:
            copy.wait_send()
        else:
            pl.when(cond)(copy.wait_send)


def body(tokens, norm_gain, qk_gain, window_blocks, w_spatial, w_temporal, w_out):
    rows, frames, width = tokens.shape
    tok = tokens.reshape(2, 64, 2, width).transpose(0, 2, 1, 3).reshape(256, width)
    vmem = pl.BlockSpec(memory_space=pltpu.VMEM)
    res = pl.pallas_call(
        kernel,
        name="attention_block",
        out_shape=pltpu.VMEM((256, width), BF16),
        in_specs=[pl.BlockSpec(memory_space=pltpu.SMEM)] + [vmem] * 6,
        out_specs=vmem,
        scratch_shapes=[
            pltpu.VMEM((256, 2048), BF16),
            pltpu.VMEM((2, 1, 128, 256), BF16),
            pltpu.VMEM((4, 512, 2048), BF16),
            pltpu.VMEM((2, 2, 2, 3, 512, 256), BF16),
            pltpu.VMEM((2, 2, 2, 1, 512, 256), BF16),
            pltpu.VMEM((2, 4, 128), F32),
            pltpu.VMEM((3, 4, 128, 16, 128), BF16),
            pltpu.VMEM((2, 4, 8, 64, 256), BF16),
            pltpu.VMEM((4, 512, 2048), BF16),
            pltpu.VMEM((4, 2, 64, 2048), BF16),
            pltpu.VMEM((4, 2, 2, 64, 2048), BF16),
            pltpu.VMEM((4, 128, 2048), BF16),
            pltpu.SemaphoreType.DMA((SLOTS,)),
            pltpu.SemaphoreType.DMA((SLOTS,)),
        ],
        compiler_params=pltpu.CompilerParams(
            collective_id=0, has_side_effects=True, vmem_limit_bytes=60 * 1024 * 1024
        ),
    )(
        window_blocks.T,
        pltpu.with_memory_space_constraint(tok, pltpu.VMEM),
        norm_gain.reshape(1, width),
        qk_gain.reshape(2, 4, 128),
        w_spatial.transpose(1, 0, 2),
        w_temporal.transpose(1, 0, 2),
        w_out,
    )
    return res.reshape(2, 2, 64, width).transpose(0, 2, 1, 3).reshape(rows, frames, width)


def solution(mesh):
    return jax.shard_map(
        body,
        mesh=mesh,
        in_specs=(
            P("grp", "seq", None),
            P(),
            P(None, None, "grp", None),
            P(),
            P("seq", None, "grp"),
            P("seq", None, "grp"),
            P("seq", None, "grp"),
        ),
        out_specs=P("grp", "seq", None),
        check_vma=False,
    )
```

```python
import jax
import jax.numpy as jnp
from jax import lax
from jax.experimental import pallas as pl
from jax.experimental.pallas import tpu as pltpu
from jax.sharding import PartitionSpec as P

MESH = pl.DeviceIdType.MESH
EPS = 1e-06
F32 = jnp.float32
BF16 = jnp.bfloat16

TOK, WGT, OUTW, GAIN, RING_TL, RING_TR, RING_W, RING_O, RS, FIN = (
    0, 4, 6, 8, 10, 16, 22, 52, 82, 106,
)
SLOTS = 110


def mm(a, b):
    return jnp.dot(a, b, preferred_element_type=F32)


def mm_t(a, b):
    return lax.dot_general(a, b, (((1,), (1,)), ((), ())), preferred_element_type=F32)


def kernel(
    win, tok, norm_gain, gain, w_s, w_t, w_o, out,
    nrm, wo_own, xs, wg, wo, gn, qkv, att, part, rs1, rs2, fin, snd, rcv,
):
    s, g = lax.axis_index("seq"), lax.axis_index("grp")
    c, y, xh = lax.rem(s, 2), lax.rem(lax.div(s, 2), 4), lax.div(s, 8)
    xl, z = lax.div(g, 4), lax.rem(g, 4)
    x = xh * 2 + xl
    nc = 1 - c
    unit = c * y + nc * z
    unit2 = nc * y + c * z
    local = nc * xl + c * xh

    def dev(xh_, y_, c_, xl_, z_):
        return ((xh_ * 4 + y_) * 2 + c_, xl_ * 4 + z_)

    def along(dy, dz):
        return dev(xh, lax.rem(y + dy, 4), c, xl, lax.rem(z + dz, 4))

    def across(dx):
        nx = lax.rem(x + dx, 4)
        return dev(lax.div(nx, 2), y, c, lax.rem(nx, 2), z)

    right, left = along(c, nc), along(3 * c, 3 * nc)
    right2, left2 = along(nc, c), along(3 * nc, 3 * c)
    right_x, left_x = across(1), across(3)

    barrier = pltpu.get_barrier_semaphore()
    peers = [right, left, right2, left2, right_x, left_x, dev(xh, y, nc, xl, z)]
    for b in range(2):
        peers.append(dev(xh, y, b, 1 - xl, z))
        peers.append(dev(1 - xh, y, b, xl, z))
        for a in range(2):
            peers.append(dev(xh, z, a, b, y))
    for to in peers:
        pl.semaphore_signal(barrier, inc=1, device_id=to, device_id_type=MESH)

    def remote(src, dst, i, j, to):
        return pltpu.make_async_remote_copy(
            src_ref=src, dst_ref=dst, send_sem=snd.at[i], recv_sem=rcv.at[j],
            device_id=to, device_id_type=MESH,
        )

    sends = []

    def put(src, dst, i, j, to):
        mine = jnp.logical_and(to[0] == s, to[1] == g)
        copy = remote(src, dst, i, j, to)

        @pl.when(mine)
        def _():
            pltpu.make_async_copy(src, dst, rcv.at[j]).start()

        @pl.when(jnp.logical_not(mine))
        def _():
            copy.start()

        sends.append((copy, jnp.logical_not(mine)))

    def arrived(dst, j):
        pltpu.make_async_copy(dst, dst, rcv.at[j]).wait()

    def start(copy):
        copy.start()
        sends.append((copy, None))

    class Ring:
        def __init__(self, view, at, to_right, to_left, base):
            self.view, self.base = view, base
            self.to = (to_right, to_left)
            self.units = (at, lax.rem(at + 3, 4), lax.rem(at + 1, 4), lax.rem(at + 2, 4))

        def send(self, u, half, k, side):
            ref = self.view(self.units[u], half)
            start(remote(ref, ref, self.base + k, self.base + k, self.to[side]))

        def wait(self, *slots):
            for k in slots:
                u, half = ((1, 0), (1, 1), (3, 0), (2, 1), (2, 0), (3, 1))[k]
                arrived(self.view(self.units[u], half), self.base + k)

        def begin(self):
            self.send(0, 0, 0, 0)
            self.send(0, 1, 3, 1)
            self.send(0, 1, 1, 0)
            self.send(0, 0, 4, 1)

        def forward(self):
            self.wait(0)
            self.send(1, 0, 2, 0)
            self.wait(3)
            self.send(2, 1, 5, 1)

        def forward_x(self):
            unit_ = (1 - xl) * self.units[2] + xl * self.units[1]
            to = tuple((1 - xl) * b + xl * a for a, b in zip(*self.to))
            for half, slot in ((0, 4 * (1 - xl)), (1, 3 - 2 * xl)):
                ref, k = self.view(unit_, half), self.base + 2 + 3 * half
                arrived(ref, self.base + slot)
                start(remote(ref, ref, k, k, to))

        def near_x(self):
            unit_ = (1 - xl) * self.units[1] + xl * self.units[2]
            for half, slot in ((0, 4 * xl), (1, 1 + 2 * xl)):
                arrived(self.view(unit_, half), self.base + slot)

    def token_ring(part_, base):
        return Ring(
            lambda u, h: xs.at[u, pl.ds((part_ * 2 + h) * 128, 128)], unit, right, left, base
        )

    def weight_rings(w, base):
        return (
            Ring(
                lambda u, h: w.at[xl, xh, 0, :, pl.ds(u * 128 + h * 64, 64)],
                unit2, right2, left2, base,
            ),
            Ring(
                lambda u, h: w.at[lax.rem(u, 2), lax.div(u, 2), 0, :, pl.ds(h * 256, 256)],
                x, right_x, left_x, base + 6,
            ),
            Ring(
                lambda u, h: w.at[
                    lax.rem(u, 2), lax.div(u, 2), 1, :, pl.ds(unit2 * 128 + h * 64, 64)
                ],
                x, right_x, left_x, base + 12,
            ),
            Ring(
                lambda u, h: w.at[1 - xl, h, 1, :, pl.ds(u * 128, 128)],
                unit2, right2, left2, base + 18,
            ),
            Ring(
                lambda u, h: w.at[xl, h, 1, :, pl.ds(u * 128, 128)],
                unit2, right2, left2, base + 24,
            ),
        )

    tok_l, tok_r = token_ring(local, RING_TL), token_ring(1 - local, RING_TR)
    w1a, w1b, w2a, w2b, w2c = weight_rings(wg, RING_W)
    o1a, o1b, o2a, o2b, o2c = weight_rings(wo, RING_O)

    def norm_half(h):
        def norm_rows(k, _):
            rows = pl.ds(pl.multiple_of(h * 128 + k * 32, 32), 32)
            v = tok[rows, :].astype(F32)
            scale = lax.rsqrt(jnp.mean(v * v, axis=-1, keepdims=True) + EPS)
            v = (v * scale * norm_gain[...]).astype(BF16)
            for old in range(16):
                new = (old // 8 * 2 + old % 2) * 4 + old // 2 % 4
                nrm[rows, new * 128 : new * 128 + 128] = v[:, old * 128 : old * 128 + 128]
            return 0

        lax.fori_loop(0, 4, norm_rows, 0)

    norm_half(0)
    norm_half(1)
    pl.semaphore_wait(barrier, len(peers))

    to_s, to_t = dev(xh, y, 0, xl, z), dev(xh, z, 1, xl, y)
    mine_w, mine_o = (w.at[xl, xh, c, :, pl.ds(y * 128, 128)] for w in (wg, wo))
    put(w_s, mine_w, WGT, WGT + c, to_s)
    put(w_t, mine_w, WGT + 1, WGT + c, to_t)
    for h in range(2):
        src = nrm.at[pl.ds(h * 128, 128)]
        i_s, i_t = xl * 2 + h, xh * 2 + c
        put(src, xs.at[z, pl.ds(i_s * 128, 128)], TOK + h, TOK + i_s, dev(xh, y, 0, c, z))
        put(src, xs.at[y, pl.ds(i_t * 128, 128)], TOK + 2 + h, TOK + i_t, dev(h, y, 1, xl, z))
    for b in range(2):
        wo_own[b, 0] = w_o[...].astype(F32)[:, b, :].astype(BF16)
    put(wo_own.at[0], mine_o, OUTW, OUTW + c, to_s)
    put(wo_own.at[1], mine_o, OUTW + 1, OUTW + c, to_t)
    for h in range(2):
        put(
            gain.at[c], gn.at[xl], GAIN + h, GAIN + xl,
            dev(xh, nc * y + c * z, c, h, nc * z + c * y),
        )

    def rows_arrived(w, i, slot):
        arrived(w.at[xl, xh, i, :, pl.ds(unit2 * 128, 128)], slot + i)

    def tokens_arrived(half):
        for h in range(2):
            i = half * 2 + h
            arrived(xs.at[unit, pl.ds(i * 128, 128)], TOK + i)

    tokens_arrived(local)
    tok_l.begin()
    rows_arrived(wg, 0, WGT)
    w1a.begin()
    rows_arrived(wg, 1, WGT)
    w2a.begin()
    tok_l.forward()
    w1a.forward()
    tokens_arrived(1 - local)
    tok_r.begin()
    w2a.forward()
    for i in range(2):
        rows_arrived(wo, i, OUTW)
    o1a.begin()
    o2a.begin()
    w1a.wait(1, 4, 2, 5)
    w1b.begin()
    w2a.wait(1, 4, 2, 5)
    w2b.begin()
    tok_r.forward()
    o1a.forward()
    o2a.forward()
    w2b.forward()
    w1b.forward_x()
    w2c.begin()
    tok_l.wait(1, 4, 2, 5)
    for i in range(2):
        arrived(gn.at[i], GAIN + i)
    tok_r.wait(1, 4, 2, 5)
    w1b.near_x()
    w2b.wait(1, 4, 2, 5)

    def project(pair, first, last):
        def one(role, u, _):
            w = [wg[pair, :, :, n].reshape(2048, 256) for n in range(3)]
            acc = mm(xs[u], jnp.concatenate(w, axis=1))
            for n in range(3):
                for j in range(2):
                    a = acc[:, n * 256 + j * 128 : n * 256 + j * 128 + 128]
                    if n < 2:
                        a = a * lax.rsqrt(jnp.mean(a * a, axis=-1, keepdims=True) + EPS)
                        a = a * gn[pair, 2 * n + j : 2 * n + j + 1, :]
                    if n == 0:
                        a = a * (128 ** -0.5)

                    if role == 0:
                        b = a.astype(BF16)
                        for k in range(8):
                            i, f = k // 2, k % 2
                            at = f * 64 + ((i // 2) * 4 + u) * 8 + i % 2 * 4
                            qkv[n, pair * 2 + j, pl.ds(at, 4)] = b[
                                k * 64 : k * 64 + 64
                            ].reshape(4, 16, 128)
                    else:
                        for i in range(4):
                            for m in range(8):
                                at = i * 128 + m * 8
                                b = jnp.concatenate([a[at : at + 8], a[at + 64 : at + 72]], axis=0)
                                at = m * 16 + ((i // 2) * 4 + u) * 2 + i % 2
                                qkv[n, pair * 2 + j, at] = b.astype(BF16)
            return 0

        for role in range(2):
            @pl.when(c == role)
            def _():
                lax.fori_loop(first, last, lambda u, v: one(role, u, v), 0)

    def softmax_mix(sc, v):
        e = jnp.exp(sc - jnp.max(sc, axis=-1, keepdims=True)).astype(BF16)
        o = mm(e, jnp.concatenate([v, jnp.ones_like(v)], axis=1))
        return o[:, 0:128] / o[:, 128:256]

    def tile(n, hd, first, rows=128):
        return qkv[n, hd, pl.ds(first, rows // 16)].reshape(rows, 128)

    def attend(pair, half, first=0, last=4):
        @pl.when(c == 0)
        def _():
            def spatial(k, _):
                k = lax.rem(unit + 2 + k, 4)
                t = half * 4 + k
                for f in range(2):
                    at = [f * 64 + win[j, t] * 8 for j in range(4)]
                    for j in range(2):
                        hd = pair * 2 + j
                        q = tile(0, hd, f * 64 + t * 8)
                        keys = jnp.concatenate([tile(1, hd, a) for a in at], axis=0)
                        vals = jnp.concatenate([tile(2, hd, a) for a in at], axis=0)
                        o = softmax_mix(mm_t(q, keys), vals).astype(BF16)
                        for h in range(2):
                            att[
                                pair, k, half * 4 + h * 2 + f, :, j * 128 : j * 128 + 128
                            ] = o[h * 64 : h * 64 + 64]
                return 0

            lax.fori_loop(first, last, spatial, 0, unroll=2 if last - first == 4 else last - first)

        for b in range(2 if first == 0 else 0):
            @pl.when(jnp.logical_and(c == 1, half == b))
            def _():
                def temporal(pg, _):
                    rows = pl.ds(pl.multiple_of(pg * 16, 16), 16)
                    keys = 128 * (b + 1)
                    qi = lax.broadcasted_iota(jnp.int32, (128, keys), 0) + b * 128
                    ki = lax.broadcasted_iota(jnp.int32, (128, keys), 1)
                    ok = jnp.logical_and(
                        jnp.bitwise_and(qi, 7) == jnp.bitwise_and(ki, 7), ki <= qi
                    )
                    for j in range(2):
                        hd = pair * 2 + j
                        res = []
                        for m in range(2):
                            first = pg * 32 + m * 16
                            q = tile(0, hd, first + b * 8)
                            sc = mm_t(q, tile(1, hd, first, keys))
                            res.append(
                                softmax_mix(jnp.where(ok, sc, -1e30), tile(2, hd, first, keys))
                            )
                        for m in range(16):
                            fr = b * 16 + m
                            i = b * 2 + (fr // 2) % 2
                            o = jnp.concatenate([v[m * 8 : m * 8 + 8] for v in res], axis=0)
                            att[
                                pair, fr // 4 % 4, i * 2 + fr % 2, rows, j * 128 : j * 128 + 128
                            ] = o.astype(BF16)
                    return 0

                lax.fori_loop(0, 4, temporal, 0, unroll=2)

    project(1 - xl, 0, 2)
    w2c.forward()
    o1a.wait(1, 4, 2, 5)
    o1b.begin()
    o2a.wait(1, 4, 2, 5)
    o2b.begin()
    o2c.begin()
    project(1 - xl, 2, 4)
    attend(1 - xl, 0)
    o1b.forward_x()
    o2b.forward()
    o2c.forward()
    attend(1 - xl, 1)
    w1b.wait(2, 5)
    w2c.wait(1, 4, 2, 5)
    project(xl, 0, 2)
    project(xl, 2, 4)
    attend(xl, 1 - local, 0, 1)
    o1b.near_x()
    o1b.wait(2, 5)
    o2b.wait(1, 4, 2, 5)
    o2c.wait(1, 4, 2, 5)

    def outproj(u, half):
        def one(k, _):
            rows = pl.ds(pl.multiple_of(half * 256, 256), 256)
            o = [att[p, u, pl.ds(half * 4, 4)].reshape(256, 256) for p in range(2)]
            for b in range(2):
                acc = mm_t(o[0], wo[0, k, b, 0]) + mm_t(o[1], wo[1, k, b, 0])
                for q in range(4):
                    cols = pl.ds(pl.multiple_of(k * 1024 + q * 256 + b * 128, 128), 128)
                    part[u, rows, cols] = acc[:, q * 128 : q * 128 + 128].astype(BF16)
            return 0

        lax.fori_loop(0, 2, one, 0)

    def add_rows(u, first, *others):
        def one(k, _):
            rows = pl.ds(pl.multiple_of(first + k * 32, 32), 32)
            here = pl.ds(pl.multiple_of(k * 32, 32), 32)
            total = part[u, rows, :].astype(F32)
            for other in others:
                total = total + other[here, :].astype(F32)
            part[u, rows, :] = total.astype(BF16)
            return 0

        lax.fori_loop(0, 2, one, 0)

    u_l, u_r, u_2 = lax.rem(unit + 3, 4), lax.rem(unit + 1, 4), lax.rem(unit + 2, 4)
    pieces = [(1 - local) * 2, (1 - local) * 2 + 1, local * 2, local * 2 + 1]

    def reduce_send(n, u, q, dst, k, to):
        src = part.at[u, pl.ds(pieces[n] * 128 + q * 64, 64)]
        start(remote(src, dst, RS + n * 6 + k, RS + n * 6 + k, to))

    def reduce_start(half, n):
        outproj(u_2, half)
        reduce_send(n, u_2, 0, rs1.at[n, 0], 0, right)
        reduce_send(n, u_2, 1, rs1.at[n, 1], 1, left)
        if n == 0:
            attend(xl, half, 1, 4)
        outproj(u_r, half)
        reduce_send(n, u_r, 1, rs2.at[n, 0, 1], 2, right)
        outproj(u_l, half)
        reduce_send(n, u_l, 0, rs2.at[n, 1, 0], 3, left)
        reduce_send(n + 1, u_2, 0, rs1.at[n + 1, 0], 0, right)
        reduce_send(n + 1, u_2, 1, rs1.at[n + 1, 1], 1, left)
        reduce_send(n + 1, u_r, 1, rs2.at[n + 1, 0, 1], 2, right)
        reduce_send(n + 1, u_l, 0, rs2.at[n + 1, 1, 0], 3, left)

    def reduce_pass(n):
        arrived(rs1.at[n, 0], RS + n * 6)
        add_rows(u_r, pieces[n] * 128, rs1.at[n, 0])
        reduce_send(n, u_r, 0, rs2.at[n, 0, 0], 4, right)
        arrived(rs1.at[n, 1], RS + n * 6 + 1)
        add_rows(u_l, pieces[n] * 128 + 64, rs1.at[n, 1])
        reduce_send(n, u_l, 1, rs2.at[n, 1, 1], 5, left)

    def reduce_end(half, n):
        h = n % 2
        for q in range(2):
            arrived(rs2.at[n, 1 - q, q], RS + n * 6 + 3 - q)
            arrived(rs2.at[n, q, q], RS + n * 6 + 4 + q)
            add_rows(unit, pieces[n] * 128 + q * 64, rs2.at[n, 0, q], rs2.at[n, 1, q])
        at = nc * h + c * (2 + xh)
        to = dev(nc * xh + c * half, y, nc * xl + c * h, nc * half + c * xl, z)
        put(part.at[unit, pl.ds(pieces[n] * 128, 128)], fin.at[at], FIN + n, FIN + at, to)

    reduce_start(1 - local, 0)
    attend(xl, local)
    reduce_pass(0)
    reduce_pass(1)
    outproj(unit, 1 - local)
    reduce_start(local, 2)
    reduce_end(1 - local, 0)
    reduce_end(1 - local, 1)
    reduce_pass(2)
    reduce_pass(3)
    outproj(unit, local)
    reduce_end(local, 2)
    reduce_end(local, 3)

    for h in range(2):
        arrived(fin.at[h], FIN + h)
        arrived(fin.at[2 + h], FIN + 2 + h)

        def total_rows(k, _):
            rows = pl.ds(pl.multiple_of(k * 32, 32), 32)
            here = pl.ds(pl.multiple_of(h * 128 + k * 32, 32), 32)
            total = fin[h, rows, :].astype(F32) + fin[2 + h, rows, :].astype(F32)
            out[here, :] = (tok[here, :].astype(F32) + total).astype(BF16)
            return 0

        lax.fori_loop(0, 4, total_rows, 0)

    for copy, cond in sends:
        if cond is None:
            copy.wait_send()
        else:
            pl.when(cond)(copy.wait_send)


def body(tokens, norm_gain, qk_gain, window_blocks, w_spatial, w_temporal, w_out):
    rows, frames, width = tokens.shape
    tok = tokens.reshape(2, 64, 2, width).transpose(0, 2, 1, 3).reshape(256, width)
    vmem = pl.BlockSpec(memory_space=pltpu.VMEM)
    res = pl.pallas_call(
        kernel,
        name="attention_block",
        out_shape=pltpu.VMEM((256, width), BF16),
        in_specs=[pl.BlockSpec(memory_space=pltpu.SMEM)] + [vmem] * 6,
        out_specs=vmem,
        scratch_shapes=[
            pltpu.VMEM((256, 2048), BF16),
            pltpu.VMEM((2, 1, 128, 256), BF16),
            pltpu.VMEM((4, 512, 2048), BF16),
            pltpu.VMEM((2, 2, 2, 3, 512, 256), BF16),
            pltpu.VMEM((2, 2, 2, 1, 512, 256), BF16),
            pltpu.VMEM((2, 4, 128), F32),
            pltpu.VMEM((3, 4, 128, 16, 128), BF16),
            pltpu.VMEM((2, 4, 8, 64, 256), BF16),
            pltpu.VMEM((4, 512, 2048), BF16),
            pltpu.VMEM((4, 2, 64, 2048), BF16),
            pltpu.VMEM((4, 2, 2, 64, 2048), BF16),
            pltpu.VMEM((4, 128, 2048), BF16),
            pltpu.SemaphoreType.DMA((SLOTS,)),
            pltpu.SemaphoreType.DMA((SLOTS,)),
        ],
        compiler_params=pltpu.CompilerParams(
            collective_id=0, has_side_effects=True, vmem_limit_bytes=60 * 1024 * 1024
        ),
    )(
        window_blocks.T,
        pltpu.with_memory_space_constraint(tok, pltpu.VMEM),
        norm_gain.reshape(1, width),
        qk_gain.reshape(2, 4, 128),
        w_spatial.transpose(1, 0, 2),
        w_temporal.transpose(1, 0, 2),
        w_out,
    )
    return res.reshape(2, 2, 64, width).transpose(0, 2, 1, 3).reshape(rows, frames, width)


def solution(mesh):
    return jax.shard_map(
        body,
        mesh=mesh,
        in_specs=(
            P("grp", "seq", None),
            P(),
            P(None, None, "grp", None),
            P(),
            P("seq", None, "grp"),
            P("seq", None, "grp"),
            P("seq", None, "grp"),
        ),
        out_specs=P("grp", "seq", None),
        check_vma=False,
    )
```
